256 devices in a mesh: wide: 32 (over z, x), narrow: 8 (over y, core).
Axes of the slice: x: 4, y: 4, z: 8, core: 2. Of those that a mesh axis runs over, the one named last changes fastest.
Arguments:
- hidden_in: bfloat16 [4096, 2048], P(('wide', 'narrow')), may hold values from -6 to 6
- queries: bfloat16 [4096, 2048], P(('wide', 'narrow')), may hold values from -6 to 6
- cache_key: bfloat16 [4096, 128, 256], P(('wide', 'narrow')), may hold values from -6 to 6
- cache_value: bfloat16 [4096, 128, 256], P(('wide', 'narrow')), may hold values from -6 to 6
- new_key: bfloat16 [4096, 256], P(('wide', 'narrow')), may hold values from -6 to 6
- new_value: bfloat16 [4096, 256], P(('wide', 'narrow')), may hold values from -6 to 6
- lengths: int32 [4096], P(('wide', 'narrow')), may hold values from 2 to 128, as said below
- norm_gain: bfloat16 [2048], replicated, may hold values from 0.5 to 1.5
- gate_codes: bfloat16 [256, 2048, 384], P(('wide', 'narrow')), may hold values from -4 to 4
- gate_scale: float32 [256, 16, 3], P(('wide', 'narrow')), may hold values from 0.011048543 to 0.044194173
- up_codes: bfloat16 [256, 2048, 384], P(('wide', 'narrow')), may hold values from -4 to 4
- up_scale: float32 [256, 16, 3], P(('wide', 'narrow')), may hold values from 0.011048543 to 0.044194173
- down_codes: bfloat16 [256, 384, 2048], P(('wide', 'narrow')), may hold values from -4 to 4
- down_scale: float32 [256, 3, 16], P(('wide', 'narrow')), may hold values from 0.018042196 to 0.07216878
- think_ids: int32 [4096, 8], P(('wide', 'narrow')), may hold values from 0 to 127, all different within a row; in each aligned block of 16 rows (0 to 15, 16 to 31, ...) at most 2 rows name the same one
- think_gates: float32 [4096, 8], P(('wide', 'narrow')), may hold values from 0.05 to 0.3
- talker_source: int32 [4096], P(('wide', 'narrow')), may hold values from 0 to 4095, as said below
- talker_gain: bfloat16 [2048], replicated, may hold values from 0.5 to 1.5
- talk_gate_w: bfloat16 [8, 2048, 384], P('narrow'), may hold values from -0.125 to 0.125
- talk_up_w: bfloat16 [8, 2048, 384], P('narrow'), may hold values from -0.125 to 0.125
- talk_down_w: bfloat16 [8, 384, 1024], P('narrow'), may hold values from -0.3125 to 0.3125
- talk_ids: int32 [4096, 2], P(('wide', 'narrow')), may hold values from 0 to 7, all different within a row; in each aligned block of 16 rows (0 to 15, 16 to 31, ...) at most 8 rows name the same one
- talk_gates: float32 [4096, 2], P(('wide', 'narrow')), may hold values from 0.3 to 0.7
Outputs:
- thinker_out: bfloat16 [4096, 2048], P(('wide', 'narrow'))
- talker_out: bfloat16 [4096, 1024], P(('wide', 'narrow'))
The draws below stay inside these ranges and needn't reach their ends.
Inputs may be any that keep to these rules, and one draw needn't show every extreme that they name: `think_ids`: each row names 8 different thinker experts; among the rows of one device no expert is named by more than 2 rows. `talk_ids`: each position names 2 different talker experts; among the positions of one device no expert is named by more than 8. `lengths`: some row uses all 128 cached positions. `talker_source`: A permutation of the rows. The row feeding a talker position lies on the same narrow index as the position. The rows of one device feed positions on exactly 16 devices, 1 positions on each.
All inputs are finite; a program needn't handle non-finite values.
Results may differ from the reference program's by a relative error of at most 0.018.
Values may be sent and summed in bfloat16 or wider, within the bound.
No kernel may reach another device: no remote copies, remote signals or barrier semaphores. Data moves between devices by JAX's collectives and lax.ppermute only.
A program may use at most 64 MiB of HBM per device.

```python
import math
import jax
import jax.numpy as jnp
import numpy as np
from jax import lax

D = 2048
HEADS = 16
KV_HEADS = 2
HEAD_DIM = 128
CTX = 128
ROWS_DEV = 16
FH = 384
BLK = 128
TOP = 8
THINK_EXP = 128
CAP = 2
TD = 1024
TF = 384
TALK_EXP = 8
TTOP = 2
TCAP = 8
RCAP = 1
ROWS = 4096
N_WIDE = 32
N_NARROW = 8


def draw_lengths(key, part):
    length_key, row_key = jax.random.split(key)
    drawn = jax.random.randint(length_key, (ROWS,), 2, CTX + 1)
    longest = jax.random.randint(row_key, (), 0, ROWS)
    return jnp.where(jnp.arange(ROWS) == longest, CTX, drawn).astype(jnp.int32)


def draw_talker_source(key, part):
    half_away = N_WIDE // 2
    before = N_WIDE - 1
    remaining = jnp.array([value for value in range(N_WIDE) if value != half_away and value != before], dtype=jnp.int32)
    columns = []
    for column in range(N_NARROW):
        shift_key, slot_key = jax.random.split(jax.random.fold_in(key, column))
        mixed = remaining[jax.random.permutation(shift_key, N_WIDE - 2)]
        leading = jnp.array([half_away, before], dtype=jnp.int32)
        shifts = jnp.concatenate([leading, mixed])[:ROWS_DEV // RCAP]
        slots = jax.random.permutation(slot_key, ROWS_DEV)
        offsets = shifts[jnp.arange(ROWS_DEV) // RCAP]
        target = jnp.arange(N_WIDE)[:, None]
        source_wide = (target + offsets[None, :]) % N_WIDE
        columns.append((source_wide * N_NARROW + column) * ROWS_DEV + slots[None, :])
    stacked = jnp.stack(columns, axis=1)
    return stacked.reshape(ROWS).astype(jnp.int32)


def background_draw(key, block_shape):
    return jax.random.truncated_normal(key, -6.0, 6.0, block_shape, jnp.float32)


def planted_heads(key):
    base_key = jax.random.fold_in(key, 9001)
    sign_key, slot_key, head_key = jax.random.split(base_key, 3)
    device_count = ROWS // ROWS_DEV
    sign_pattern = jnp.where(jax.random.bernoulli(sign_key, 0.5, (ROWS, HEAD_DIM)), 1.0, -1.0).astype(jnp.float32)
    chosen_slot = jax.random.randint(slot_key, (device_count,), 0, ROWS_DEV)
    chosen_head = jax.random.randint(head_key, (device_count,), 0, HEADS)
    row_index = jnp.arange(ROWS)
    row_owner = row_index // ROWS_DEV
    marked = row_index % ROWS_DEV == chosen_slot[row_owner]
    strength = 4.0 + (row_owner % 3).astype(jnp.float32)
    return (marked, strength, chosen_head[row_owner], sign_pattern)


def draw_queries(key, part):
    marked, strength, head_of, sign_pattern = planted_heads(key)
    background = background_draw(jax.random.fold_in(key, 11), (ROWS, HEADS, HEAD_DIM))
    aimed = marked[:, None] & (jnp.arange(HEADS)[None, :] == head_of[:, None])
    planted = strength[:, None, None] * sign_pattern[:, None, :]
    filled = jnp.where(aimed[:, :, None], planted, background)
    return filled.reshape(ROWS, HEADS * HEAD_DIM).astype(jnp.bfloat16)


def draw_cache_key(key, part):
    marked, strength, head_of, sign_pattern = planted_heads(key)
    background = background_draw(jax.random.fold_in(key, 12), (ROWS, CTX, KV_HEADS, HEAD_DIM))
    key_group = head_of // (HEADS // KV_HEADS)
    nearer = strength - 2.0 / (strength * HEAD_DIM ** 0.5)
    places = jnp.arange(CTX)
    level = jnp.where(places[None, :] == 0, strength[:, None], nearer[:, None])
    in_group = jnp.arange(KV_HEADS)[None, :] == key_group[:, None]
    aimed = marked[:, None, None] & (places < 2)[None, :, None] & in_group[:, None, :]
    planted = level[:, :, None, None] * sign_pattern[:, None, None, :]
    filled = jnp.where(aimed[:, :, :, None], planted, background)
    return filled.reshape(ROWS, CTX, KV_HEADS * HEAD_DIM).astype(jnp.bfloat16)


def level_of(key, extent, pieces, smallest, top_value):
    loudness, own = 1.0, jax.random.fold_in(key, 6)
    for axis_at, blocks in pieces:
        steps = jnp.exp(jax.random.uniform(jax.random.fold_in(own, axis_at), (blocks,), jnp.float32, smallest / len(pieces), top_value / len(pieces)))
        loudness = loudness * jnp.repeat(steps, extent[axis_at] // blocks).reshape([-1 if axis == axis_at else 1 for axis in range(len(extent))])
    return loudness


def routed_block(stream_key, own, number, rows, count, top, most, lean):
    order = jax.random.permutation(stream_key, count)
    crowded, common = portions_of(count, rows * top, most, lean, True), portions_of(count, rows * top, most, lean, False)
    places = jnp.arange(count)

    def named(tallies, offset_by):
        used = int((tallies > 0).sum())
        fixed = max(1, used // 4)
        shifted = fixed + (places - fixed + offset_by * (used - fixed)) % max(1, count - fixed)
        return jnp.zeros((count,), jnp.int32).at[order[jnp.where(places < fixed, places, shifted)]].set(jnp.asarray(tallies, jnp.int32))

    tallies = jnp.where(number % 4 == 0, named(crowded, number // 4), named(common, number - number // 4 - 1))
    mixed = jax.random.permutation(jax.random.fold_in(own, 3), count)
    giver, sink = mixed[0:count // 2 * 2:2], mixed[1:count // 2 * 2:2]
    room = jnp.minimum(tallies[giver] - 1, most - tallies[sink]) // 2
    room = jnp.where((giver == order[0]) | (sink == order[0]) | (tallies[sink] == 0), 0, jnp.maximum(room, 0))
    shifted = jax.random.randint(jax.random.fold_in(own, 4), (count // 2,), 0, 1 << 20) % (room + 1)
    tallies = tallies.at[giver].add(-shifted).at[sink].add(shifted)
    members = jnp.searchsorted(jnp.cumsum(tallies), jnp.arange(rows * top), side="right").astype(jnp.int32)
    grid = members.reshape(top, rows).T
    grid = grid[jax.random.permutation(jax.random.fold_in(own, 1), rows)]
    offset_by = jax.random.randint(jax.random.fold_in(own, 2), (rows, 1), 0, top)
    return jnp.take_along_axis(grid, (jnp.arange(top)[None, :] + offset_by) % top, axis=1)


def portions_of(count, total, reach, lean, full):
    loads = [(1 << 20) // math.isqrt(grade ** lean) + 1 for grade in range(1, count + 1)]
    largest = reach if full else min(reach, max(-(-total // count), total * loads[0] // sum(loads)))
    least = 1 if total - largest >= count - 1 else 0
    counts, spare = [largest] + [least] * (count - 1), total - largest - least * (count - 1)
    while spare > 0:
        candidates = [i for i in range(1, count) if counts[i] < largest] or [i for i in range(1, count) if counts[i] < reach]
        pool, left = sum([loads[i] for i in candidates]), spare
        for i in candidates:
            addition = min(reach - counts[i], max(1, left * loads[i] // pool), spare)
            counts[i] = counts[i] + addition
            spare = spare - addition
    return np.array(counts)


def centred(stream_key, shape, scale, bound, shards=(), held_as=jnp.bfloat16):
    entries = scale * jax.random.normal(stream_key, shape, jnp.float32)
    if shards:
        entries = entries * level_of(stream_key, shape, shards, -0.22, 0.18)
    return jnp.clip(entries, -bound, bound).astype(held_as)


def setup_inputs(seed: int = 0) -> dict:
    splits = jax.random.split(jax.random.key(seed), 24)
    hidden_in = centred(splits[0], (ROWS, D), 1.0, 6.0, ((0, 256),))
    queries = draw_queries(jax.random.fold_in(splits[23], 71), 0)
    cache_key = draw_cache_key(jax.random.fold_in(splits[23], 71), 0)
    cache_value = centred(splits[3], (ROWS, CTX, KV_HEADS * HEAD_DIM), 1.0, 6.0, ((0, 256),))
    new_key = centred(splits[4], (ROWS, KV_HEADS * HEAD_DIM), 1.0, 6.0, ((0, 256),))
    new_value = centred(splits[5], (ROWS, KV_HEADS * HEAD_DIM), 1.0, 6.0, ((0, 256),))
    lengths = draw_lengths(jax.random.fold_in(splits[23], 71), 0)
    norm_gain = jnp.clip(1.0 + 0.1 * jax.random.normal(splits[7], (D,), jnp.float32), 0.5, 1.5).astype(jnp.bfloat16)
    gate_codes = centred(splits[8], (2 * THINK_EXP, D, FH), 1.0, 4.0, ((0, 256),))
    gate_scale = jnp.clip(jnp.exp(math.log(0.044194173) - 1.3862944 * jax.random.uniform(splits[9], (2 * THINK_EXP, D // BLK, FH // BLK), jnp.float32) ** level_of(splits[9], (2 * THINK_EXP, D // BLK, FH // BLK), ((0, 256),), -0.2, 0.2)), 0.011048543, 0.044194173)
    up_codes = centred(splits[10], (2 * THINK_EXP, D, FH), 1.0, 4.0, ((0, 256),))
    up_scale = jnp.clip(jnp.exp(math.log(0.044194173) - 1.3862944 * jax.random.uniform(splits[11], (2 * THINK_EXP, D // BLK, FH // BLK), jnp.float32) ** level_of(splits[11], (2 * THINK_EXP, D // BLK, FH // BLK), ((0, 256),), -0.2, 0.2)), 0.011048543, 0.044194173)
    down_codes = centred(splits[12], (2 * THINK_EXP, FH, D), 1.0, 4.0, ((0, 256),))
    down_scale = jnp.clip(jnp.exp(math.log(0.07216878) - 1.3862944 * jax.random.uniform(splits[13], (2 * THINK_EXP, FH // BLK, D // BLK), jnp.float32) ** level_of(splits[13], (2 * THINK_EXP, FH // BLK, D // BLK), ((0, 256),), -0.2, 0.2)), 0.018042196, 0.07216878)
    think_ids_keys = jax.random.split(jax.random.fold_in(splits[14], 1), ROWS // ROWS_DEV)
    think_ids_turns = jax.random.permutation(jax.random.fold_in(splits[14], 3), ROWS // ROWS_DEV)
    think_ids = jax.vmap(lambda own, number: routed_block(jax.random.fold_in(splits[14], 2), own, number, ROWS_DEV, THINK_EXP, TOP, CAP, 2))(think_ids_keys, think_ids_turns).reshape((ROWS, TOP))
    think_gates = jnp.clip(0.05 + 0.25 * jax.random.uniform(splits[15], (ROWS, TOP), jnp.float32) ** level_of(splits[15], (ROWS, TOP), ((0, 256),), -0.2, 0.2), 0.05, 0.3)
    talker_source = draw_talker_source(jax.random.fold_in(splits[23], 71), 0)
    talker_gain = jnp.clip(1.0 + 0.1 * jax.random.normal(splits[17], (D,), jnp.float32), 0.5, 1.5).astype(jnp.bfloat16)
    talk_gate_w = centred(splits[18], (TALK_EXP, D, TF), D ** -0.5, 0.125, ((0, 8),))
    talk_up_w = centred(splits[19], (TALK_EXP, D, TF), D ** -0.5, 0.125, ((0, 8),))
    talk_down_w = centred(splits[20], (TALK_EXP, TF, TD), TF ** -0.5, 0.3125, ((0, 8),))
    talk_ids_keys = jax.random.split(jax.random.fold_in(splits[21], 1), ROWS // ROWS_DEV)
    talk_ids_turns = jax.random.permutation(jax.random.fold_in(splits[21], 3), ROWS // ROWS_DEV)
    talk_ids = jax.vmap(lambda own, number: routed_block(jax.random.fold_in(splits[21], 2), own, number, ROWS_DEV, TALK_EXP, TTOP, TCAP, 1))(talk_ids_keys, talk_ids_turns).reshape((ROWS, TTOP))
    talk_gates = jnp.clip(0.3 + 0.39999998 * jax.random.uniform(splits[22], (ROWS, TTOP), jnp.float32) ** level_of(splits[22], (ROWS, TTOP), ((0, 256),), -0.2, 0.2), 0.3, 0.7)
    return {"hidden_in": hidden_in, "queries": queries, "cache_key": cache_key, "cache_value": cache_value, "new_key": new_key, "new_value": new_value, "lengths": lengths, "norm_gain": norm_gain, "gate_codes": gate_codes, "gate_scale": gate_scale, "up_codes": up_codes, "up_scale": up_scale, "down_codes": down_codes, "down_scale": down_scale, "think_ids": think_ids, "think_gates": think_gates, "talker_source": talker_source, "talker_gain": talker_gain, "talk_gate_w": talk_gate_w, "talk_up_w": talk_up_w, "talk_down_w": talk_down_w, "talk_ids": talk_ids, "talk_gates": talk_gates}


EPSILON = 1e-06

def dequantize(code_block, scale_block):
    height, breadth = code_block.shape
    tiles = code_block.astype(jnp.float32).reshape(height // BLK, BLK, breadth // BLK, BLK)
    tiles = tiles * scale_block.astype(jnp.float32)[:, None, :, None]
    return tiles.reshape(height, breadth).astype(jnp.bfloat16)

def rms_norm(values, gain):
    values = values.astype(jnp.float32)
    spread = lax.optimization_barrier(jnp.mean(values * values, axis=-1, keepdims=True))
    return (values * lax.rsqrt(spread + EPSILON) * gain.astype(jnp.float32)).astype(jnp.bfloat16)

def swiglu(inputs, gate_dense, up_dense, down_dense):
    gated = jnp.dot(inputs, gate_dense, preferred_element_type=jnp.float32)
    lifted = jnp.dot(inputs, up_dense, preferred_element_type=jnp.float32)
    middle = (jax.nn.silu(gated) * lifted).astype(jnp.bfloat16)
    return jnp.dot(middle, down_dense, preferred_element_type=jnp.float32).astype(jnp.bfloat16)

def attend(queries, cache_key, cache_value, new_key, new_value, lengths):
    row_count = queries.shape[0]
    groups = HEADS // KV_HEADS
    scaling = HEAD_DIM ** (-0.5)
    asked = queries.astype(jnp.float32).reshape(row_count, KV_HEADS, groups, HEAD_DIM)
    cached_keys = cache_key.astype(jnp.float32).reshape(row_count, CTX, KV_HEADS, HEAD_DIM)
    cached_values = cache_value.astype(jnp.float32).reshape(row_count, CTX, KV_HEADS, HEAD_DIM)
    scores = jnp.einsum('rkgd,rtkd->rkgt', asked, cached_keys) * scaling
    fresh_score = jnp.einsum('rkgd,rkd->rkg', asked, new_key.astype(jnp.float32).reshape(row_count, KV_HEADS, HEAD_DIM)) * scaling
    places = jnp.arange(CTX, dtype=jnp.int32)
    live_mask = places[None, :] < lengths[:, None]
    scores = jnp.where(live_mask[:, None, None, :], scores, -jnp.inf)
    highest = jnp.maximum(lax.optimization_barrier(jnp.max(scores, axis=-1)), fresh_score)
    weights = jnp.exp(scores - highest[..., None])
    own_weight = jnp.exp(fresh_score - highest)
    totals = lax.optimization_barrier(jnp.sum(weights, axis=-1)) + own_weight
    probabilities = (weights / totals[..., None]).astype(jnp.bfloat16)
    own_prob = (own_weight / totals).astype(jnp.bfloat16)
    mixture = jnp.einsum('rkgt,rtkd->rkgd', probabilities.astype(jnp.float32), cached_values)
    newest = new_value.astype(jnp.float32).reshape(row_count, KV_HEADS, 1, HEAD_DIM)
    mixture = mixture + own_prob.astype(jnp.float32)[..., None] * newest
    return mixture.reshape(row_count, HEADS * HEAD_DIM)

def routed_sum(inputs, expert_ids, gate_weights, expert_count, limit, expert_fn, breadth):
    chosen = expert_ids[:, :, None] == jnp.arange(expert_count, dtype=jnp.int32)[None, None, :]
    picked = jnp.any(chosen, axis=1)
    weight_of = lax.optimization_barrier(jnp.sum(jnp.where(chosen, gate_weights.astype(jnp.float32)[:, :, None], jnp.float32(0.0)), axis=1))

    def add_expert(running, expert):
        column = picked[:, expert]
        indices = jnp.nonzero(column, size=limit, fill_value=0)[0].astype(jnp.int32)
        count = jnp.sum(column.astype(jnp.int32))
        valid = jnp.arange(limit, dtype=jnp.int32) < count
        scales = jnp.where(valid, weight_of[indices, expert], jnp.float32(0.0))
        result = expert_fn(expert, inputs[indices])
        return (running.at[indices].add(result * scales[:, None]), None)
    start = jnp.zeros((inputs.shape[0], breadth), jnp.float32)
    running, unused = lax.scan(add_expert, start, jnp.arange(expert_count, dtype=jnp.int32))
    return running

def reference(hidden_in, queries, cache_key, cache_value, new_key, new_value, lengths, norm_gain, gate_codes, gate_scale, up_codes, up_scale, down_codes, down_scale, think_ids, think_gates, talker_source, talker_gain, talk_gate_w, talk_up_w, talk_down_w, talk_ids, talk_gates):
    attended = attend(queries, cache_key, cache_value, new_key, new_value, lengths)
    residual = hidden_in.astype(jnp.float32) + attended
    normed = rms_norm(residual, norm_gain)

    def thinker_expert(expert, rows_in):
        output = jnp.zeros((rows_in.shape[0], D), jnp.float32)
        for half in range(2):
            index = 2 * expert + half
            gate_dense = dequantize(gate_codes[index], gate_scale[index])
            up_dense = dequantize(up_codes[index], up_scale[index])
            down_dense = dequantize(down_codes[index], down_scale[index])
            output = output + swiglu(rows_in, gate_dense, up_dense, down_dense).astype(jnp.float32)
        return output
    limit = min(ROWS, CAP * N_WIDE * N_NARROW)
    routed = routed_sum(normed, think_ids, think_gates, THINK_EXP, limit, thinker_expert, D)
    thinker_out = (residual + routed).astype(jnp.bfloat16)
    talker_in = thinker_out[talker_source]
    talker_normed = rms_norm(talker_in, talker_gain)

    def talker_expert(expert, rows_in):
        return swiglu(rows_in, talk_gate_w[expert], talk_up_w[expert], talk_down_w[expert]).astype(jnp.float32)
    talk_limit = min(ROWS, TCAP * N_WIDE * N_NARROW)
    talked = routed_sum(talker_normed, talk_ids, talk_gates, TALK_EXP, talk_limit, talker_expert, TD)
    return (thinker_out, talked.astype(jnp.bfloat16))
```

```python
import functools

import jax
import jax.numpy as jnp
from jax import lax
from jax.experimental import pallas as pl
from jax.experimental.pallas import tpu as pltpu
from jax.sharding import Mesh
from jax.sharding import PartitionSpec as P

HEADS = 16
HEAD_DIM = 128
BLK = 128
CHIPS = 128
LANES = 128
ROWS = 16
CTX = 128
D = 2048
FH = 384
TD = 1024
EPSILON = 1e-06
MSG = 40
INFO_ROW = 32
TWIDE = D + 2 * LANES

f32 = jnp.float32
bf16 = jnp.bfloat16
VM = pl.BlockSpec(memory_space=pltpu.VMEM)
SM = pl.BlockSpec(memory_space=pltpu.SMEM)
HB = pl.BlockSpec(memory_space=pl.ANY)


def lane_iota(rows):
    return lax.broadcasted_iota(jnp.int32, (rows, LANES), 1)


def slots(ids):
    lane = lane_iota(ROWS)
    picked = jnp.zeros((ROWS, LANES), f32)
    for k in range(ids.shape[1]):
        picked = picked + jnp.where(ids[:, k : k + 1] == lane, 1.0, 0.0)
    below = lax.broadcasted_iota(jnp.int32, (ROWS, ROWS), 1) < lax.broadcasted_iota(
        jnp.int32, (ROWS, ROWS), 0
    )
    rank = jnp.dot(
        jnp.where(below, 1.0, 0.0).astype(bf16), picked.astype(bf16), preferred_element_type=f32
    )
    first = jnp.where((picked > 0.5) & (rank < 0.5), 1.0, 0.0)
    second = jnp.where((picked > 0.5) & (rank > 0.5) & (rank < 1.5), 1.0, 0.0)
    return first, second


def high_low(values):
    high = values.astype(bf16)
    low = (values - high.astype(f32)).astype(bf16)
    return high, low


def gather_t(onehot, values):
    return lax.dot_general(
        onehot, values, (((0,), (0,)), ((), ())), preferred_element_type=f32
    )


def attend_kernel(
    hidden, queries, cache_key, cache_value, new_key, new_value, lengths, gain, ids,
    source, talk_ids, talk_gates, residual, message, asked, mixed, spread_out,
):
    scaling = HEAD_DIM ** (-0.5)
    for h in range(HEADS):
        asked[pl.ds(h, ROWS, stride=HEADS), :] = queries[:, h * 128 : (h + 1) * 128].astype(f32)
    head = lax.broadcasted_iota(jnp.int32, (HEADS, LANES), 0)
    front = head < HEADS // 2
    lane = lane_iota(HEADS)
    fresh_key = new_key[...].astype(f32)
    fresh_value = new_value[...].astype(f32)
    for r in range(ROWS):
        query = asked[r * HEADS : (r + 1) * HEADS, :]
        split = jnp.concatenate(
            [jnp.where(front, query, 0.0), jnp.where(front, 0.0, query)], axis=1
        ).astype(bf16)
        scores = (
            lax.dot_general(
                split, cache_key[r], (((1,), (1,)), ((), ())), preferred_element_type=f32
            )
            * scaling
        )
        own_key = jnp.where(front, fresh_key[r : r + 1, :128], fresh_key[r : r + 1, 128:])
        own_val = jnp.where(front, fresh_value[r : r + 1, :128], fresh_value[r : r + 1, 128:])
        fresh = jnp.sum(query * own_key, axis=1, keepdims=True) * scaling
        scores = jnp.where(lane < lengths[r], scores, -jnp.inf)
        highest = jnp.maximum(jnp.max(scores, axis=1, keepdims=True), fresh)
        weights = jnp.exp(scores - highest)
        own = jnp.exp(fresh - highest)
        total = jnp.sum(weights, axis=1, keepdims=True) + own
        probs = (weights / total).astype(bf16)
        own_prob = (own / total).astype(bf16).astype(f32)
        both = jnp.dot(probs, cache_value[r], preferred_element_type=f32)
        mixed[r * HEADS : (r + 1) * HEADS, :] = (
            jnp.where(front, both[:, :128], both[:, 128:]) + own_prob * own_val
        )
    squares = jnp.zeros((ROWS, LANES), f32)
    for h in range(HEADS):
        cols = slice(h * 128, (h + 1) * 128)
        part = hidden[:, cols].astype(f32) + mixed[pl.ds(h, ROWS, stride=HEADS), :]
        residual[:, cols] = part
        squares = squares + part * part
    spread = jnp.sum(squares, axis=1, keepdims=True) * (1.0 / D)
    scale = lax.rsqrt(spread + EPSILON)
    first, second = slots(ids[...])
    first, second = first.astype(bf16), second.astype(bf16)
    for h in range(HEADS):
        cols = slice(h * 128, (h + 1) * 128)
        normed = (residual[:, cols] * scale * gain[:, cols].astype(f32)).astype(bf16)
        spread_out[pl.ds(h, CHIPS, stride=32), :] = gather_t(first, normed)
        spread_out[pl.ds(HEADS + h, CHIPS, stride=32), :] = gather_t(second, normed)
    message[:, :INFO_ROW, :] = spread_out[...].reshape(CHIPS, 32, LANES).astype(bf16)
    lane = lane_iota(ROWS)
    origin = source[...]
    onehot = jnp.where((origin // 32) == lane, 1.0, 0.0).astype(bf16)
    gates = talk_gates[...]
    high = gates.astype(bf16).astype(f32)
    low = gates - high
    facts = jnp.where(lane == 16 + origin % ROWS, 1.0, 0.0)
    for k in range(2):
        chosen = talk_ids[:, k : k + 1]
        facts = facts + jnp.where(lane == chosen, high[:, k : k + 1], 0.0)
        facts = facts + jnp.where(lane == chosen + 8, low[:, k : k + 1], 0.0)
    told = gather_t(onehot, facts.astype(bf16)).astype(bf16)
    message[:, INFO_ROW:, :] = jnp.broadcast_to(
        told.astype(f32).reshape(CHIPS, 1, LANES), (CHIPS, MSG - INFO_ROW, LANES)
    ).astype(bf16)


def silu(x):
    return x * jax.nn.sigmoid(x)


def expert_kernel(
    arrived, gs0, us0, ds0, gs1, us1, ds1, g0, u0, d0, g1, u1, d1, produced, info,
    wide_in, rows_in, gw, uw, dw, out32, sems,
):
    copies = []
    for i, (src, dst) in enumerate(
        [
            (g0, gw.at[0]), (u0, uw.at[0]), (d0, dw.at[0]),
            (g1, gw.at[1]), (u1, uw.at[1]), (d1, dw.at[1]),
        ]
    ):
        copy = pltpu.make_async_copy(src.at[0], dst, sems.at[i])
        copy.start()
        copies.append(copy)
    wide_in[...] = arrived[...].astype(f32).reshape(CHIPS * MSG, LANES)
    info[...] = wide_in[pl.ds(INFO_ROW, CHIPS, stride=MSG), :].astype(bf16)
    for s in range(2):
        for h in range(HEADS):
            rows_in[s * CHIPS : (s + 1) * CHIPS, h * 128 : (h + 1) * 128] = wide_in[
                pl.ds(s * HEADS + h, CHIPS, stride=MSG), :
            ].astype(bf16)

    def dequantize(weights, half, scales, tall, broad):
        for j in range(broad):
            cols = slice(j * BLK, (j + 1) * BLK)

            def step(i, carry):
                start = pl.multiple_of(i * BLK, BLK)
                block = weights[half, pl.ds(start, BLK), cols].astype(f32) * scales[0, i, j]
                weights[half, pl.ds(start, BLK), cols] = block.astype(bf16)
                return carry

            lax.fori_loop(0, tall, step, 0)

    total = None
    for half, (gs, us, ds) in enumerate([(gs0, us0, ds0), (gs1, us1, ds1)]):
        copies[3 * half].wait()
        dequantize(gw, half, gs, D // BLK, FH // BLK)
        gated = jnp.dot(rows_in[...], gw[half], preferred_element_type=f32)
        copies[3 * half + 1].wait()
        dequantize(uw, half, us, D // BLK, FH // BLK)
        lifted = jnp.dot(rows_in[...], uw[half], preferred_element_type=f32)
        middle = (silu(gated) * lifted).astype(bf16)
        copies[3 * half + 2].wait()
        dequantize(dw, half, ds, FH // BLK, D // BLK)
        for h in range(HEADS):
            cols = slice(h * 128, (h + 1) * 128)
            part = jnp.dot(middle, dw[half, :, cols], preferred_element_type=f32)
            part = part.astype(bf16).astype(f32)
            for s in range(2):
                spot = pl.ds(s * HEADS + h, CHIPS, stride=32)
                rows = part[s * CHIPS : (s + 1) * CHIPS]
                if half == 0:
                    out32[spot, :] = rows
                else:
                    out32[spot, :] = out32[spot, :] + rows
    produced[...] = out32[...].reshape(CHIPS, 32, LANES).astype(bf16)


def combine_kernel(
    returned, residual, ids, gates, info, gain, thinker_out, onward, wide_in, rows_in,
):
    wide_in[...] = returned[...].astype(f32).reshape(CHIPS * 32, LANES)
    for s in range(2):
        for h in range(HEADS):
            rows_in[s * CHIPS : (s + 1) * CHIPS, h * 128 : (h + 1) * 128] = wide_in[
                pl.ds(s * HEADS + h, CHIPS, stride=32), :
            ].astype(bf16)
    lane = lane_iota(ROWS)
    weight = jnp.zeros((ROWS, LANES), f32)
    for k in range(8):
        weight = weight + jnp.where(ids[:, k : k + 1] == lane, gates[:, k : k + 1], 0.0)
    first, second = slots(ids[...])
    high, low = high_low(jnp.concatenate([first * weight, second * weight], axis=1))
    routed = jnp.dot(high, rows_in[...], preferred_element_type=f32) + jnp.dot(
        low, rows_in[...], preferred_element_type=f32
    )
    outcome = (residual[...] + routed).astype(bf16)
    thinker_out[...] = outcome
    values = outcome.astype(f32)
    spread = jnp.sum(values * values, axis=1, keepdims=True) * (1.0 / D)
    onward[:, :D] = (values * lax.rsqrt(spread + EPSILON) * gain[...].astype(f32)).astype(bf16)
    told = info[...]
    pick = jnp.where(
        lane == 16 + lax.broadcasted_iota(jnp.int32, (ROWS, LANES), 0), 1.0, 0.0
    ).astype(bf16)
    goal = lax.dot_general(
        pick, told, (((1,), (1,)), ((), ())), preferred_element_type=f32
    ).astype(bf16)
    onward[:, D : D + LANES] = goal
    onward[:, D + LANES :] = jnp.dot(goal, told, preferred_element_type=f32).astype(bf16)


def talker_kernel(
    place, m0, m1, m2, m3, g0, u0, d0, g1, u1, d1, relayed, rows_in, gw, uw, dw, out32, sems,
):
    copies = []
    for i, (src, dst) in enumerate(
        [
            (g0, gw.at[0]), (u0, uw.at[0]), (d0, dw.at[0]),
            (g1, gw.at[1]), (u1, uw.at[1]), (d1, dw.at[1]),
        ]
    ):
        copy = pltpu.make_async_copy(src.at[0], dst, sems.at[i])
        copy.start()
        copies.append(copy)
    for i, m in enumerate([m0, m1, m2, m3]):
        rows_in[i * ROWS : (i + 1) * ROWS, :] = m[...]
    inputs = rows_in[:, :D]
    goal = rows_in[:, D : D + LANES]
    shares = rows_in[:, D + LANES :].astype(f32)
    lane = lane_iota(4 * ROWS)
    total = jnp.zeros((4 * ROWS, TD), f32)
    for half in range(2):
        expert = place[0] if half == 0 else place[0] + 1 - 2 * (place[0] % 2)
        share = jnp.sum(
            jnp.where((lane == expert) | (lane == expert + 8), shares, 0.0), axis=1, keepdims=True
        )
        copies[3 * half].wait()
        gated = jnp.dot(inputs, gw[half], preferred_element_type=f32)
        copies[3 * half + 1].wait()
        lifted = jnp.dot(inputs, uw[half], preferred_element_type=f32)
        middle = (silu(gated) * lifted).astype(bf16)
        copies[3 * half + 2].wait()
        part = jnp.dot(middle, dw[half], preferred_element_type=f32)
        total = total + share * part.astype(bf16).astype(f32)
    total = total.astype(bf16)
    for h in range(TD // 128):
        out32[pl.ds(h, CHIPS, stride=8), :] = gather_t(goal, total[:, h * 128 : (h + 1) * 128])
    relayed[...] = out32[...].reshape(CHIPS, 8, LANES).astype(bf16)


def settle_kernel(returned, source, talker_out, wide_in):
    wide_in[...] = returned[...].astype(f32).reshape(CHIPS * 8, LANES)
    lane = lane_iota(ROWS)
    onehot = jnp.where((lane // 4) == (source[...] // 128), 1.0, 0.0).astype(bf16)
    for h in range(TD // 128):
        rows = wide_in[pl.ds(h, CHIPS, stride=8), :].astype(bf16)
        talker_out[:, h * 128 : (h + 1) * 128] = jnp.dot(
            onehot, rows, preferred_element_type=f32
        ).astype(bf16)


def params(mib):
    return pltpu.CompilerParams(vmem_limit_bytes=mib * 1024 * 1024)


def sds(shape, dtype):
    return jax.ShapeDtypeStruct(shape, dtype)


def swap(value):
    return lax.ppermute(value, "c", [(0, 1), (1, 0)])


def spread_chips(value):
    return lax.all_to_all(value, ("z", "x", "y"), 0, 0, tiled=True)


def local(
    hidden_in, queries, cache_key, cache_value, new_key, new_value, lengths, norm_gain,
    gate_codes, gate_scale, up_codes, up_scale, down_codes, down_scale, think_ids, think_gates,
    talker_source, talker_gain, talk_gate_w, talk_up_w, talk_down_w, talk_ids, talk_gates,
):
    own = (gate_codes, up_codes, down_codes)
    other = tuple(swap(w) for w in own)
    own_scale = (gate_scale, up_scale, down_scale)
    other_scale = tuple(swap(s) for s in own_scale)
    talk_own = (talk_gate_w, talk_up_w, talk_down_w)
    talk_other = tuple(swap(w) for w in talk_own)
    source = talker_source.reshape(ROWS, 1)

    residual, message = pl.pallas_call(
        attend_kernel,
        out_shape=(sds((ROWS, D), f32), sds((CHIPS, MSG, LANES), bf16)),
        in_specs=[VM] * 6 + [SM] + [VM] * 5,
        out_specs=(VM, VM),
        scratch_shapes=[
            pltpu.VMEM((ROWS * HEADS, LANES), f32),
            pltpu.VMEM((ROWS * HEADS, LANES), f32),
            pltpu.VMEM((CHIPS * 32, LANES), f32),
        ],
        compiler_params=params(24),
        name="attend",
    )(
        hidden_in, queries, cache_key, cache_value, new_key, new_value, lengths,
        norm_gain.reshape(1, D), think_ids, source, talk_ids, talk_gates,
    )
    arrived = spread_chips(message)
    produced, info = pl.pallas_call(
        expert_kernel,
        out_shape=(sds((CHIPS, 32, LANES), bf16), sds((CHIPS, LANES), bf16)),
        in_specs=[VM] + [SM] * 6 + [HB] * 6,
        out_specs=(VM, VM),
        scratch_shapes=[
            pltpu.VMEM((CHIPS * MSG, LANES), f32),
            pltpu.VMEM((2 * CHIPS, D), bf16),
            pltpu.VMEM((2, D, FH), bf16),
            pltpu.VMEM((2, D, FH), bf16),
            pltpu.VMEM((2, FH, D), bf16),
            pltpu.VMEM((CHIPS * 32, LANES), f32),
            pltpu.SemaphoreType.DMA((6,)),
        ],
        compiler_params=params(40),
        name="experts",
    )(arrived, *own_scale, *other_scale, *own, *other)
    returned = spread_chips(produced)
    thinker_out, onward = pl.pallas_call(
        combine_kernel,
        out_shape=(sds((ROWS, D), bf16), sds((ROWS, TWIDE), bf16)),
        in_specs=[VM] * 6,
        out_specs=(VM, VM),
        scratch_shapes=[
            pltpu.VMEM((CHIPS * 32, LANES), f32),
            pltpu.VMEM((2 * CHIPS, D), bf16),
        ],
        compiler_params=params(24),
        name="combine",
    )(returned, residual, think_ids, think_gates, info, talker_gain.reshape(1, D))
    peers = [
        lax.ppermute(onward, "y", [(i, (i + o) % 4) for i in range(4)]) for o in (1, 2, 3)
    ]
    place = (lax.axis_index("y") * 2 + lax.axis_index("c")).astype(jnp.int32).reshape(1)
    relayed = pl.pallas_call(
        talker_kernel,
        out_shape=sds((CHIPS, 8, LANES), bf16),
        in_specs=[SM] + [VM] * 4 + [HB] * 6,
        out_specs=VM,
        scratch_shapes=[
            pltpu.VMEM((4 * ROWS, TWIDE), bf16),
            pltpu.VMEM((2, D, FH), bf16),
            pltpu.VMEM((2, D, FH), bf16),
            pltpu.VMEM((2, FH, TD), bf16),
            pltpu.VMEM((CHIPS * 8, LANES), f32),
            pltpu.SemaphoreType.DMA((6,)),
        ],
        compiler_params=params(32),
        name="talkers",
    )(place, onward, *peers, *talk_own, *talk_other)
    settled = spread_chips(relayed)
    talker_out = pl.pallas_call(
        settle_kernel,
        out_shape=sds((ROWS, TD), bf16),
        in_specs=[VM, VM],
        out_specs=VM,
        scratch_shapes=[pltpu.VMEM((CHIPS * 8, LANES), f32)],
        compiler_params=params(16),
        name="settle",
    )(settled, source)
    return (thinker_out, talker_out)


def solution(mesh):
    fine = Mesh(mesh.devices.reshape(8, 4, 4, 2), ("z", "x", "y", "c"))
    every = ("z", "x", "y", "c")
    two = P(every, None)
    three = P(every, None, None)
    talk = P(("y", "c"), None, None)
    return jax.shard_map(
        local,
        mesh=fine,
        in_specs=(
            two, two, three, three, two, two, P(every), P(),
            three, three, three, three, three, three, two, two,
            P(every), P(), talk, talk, talk, two, two,
        ),
        out_specs=(two, two),
        check_vma=False,
    )
```

```python
import jax
import jax.numpy as jnp
from jax import lax
from jax.experimental import pallas as pl
from jax.experimental.pallas import tpu as pltpu
from jax.sharding import Mesh
from jax.sharding import PartitionSpec as P

HEADS = 16
HEAD_DIM = 128
BLK = 128
CHIPS = 128
LANES = 128
ROWS = 16
CTX = 128
D = 2048
FH = 384
TD = 1024
EPSILON = 1e-06
MSG = 40
INFO_ROW = 32
TWIDE = D + 2 * LANES

f32 = jnp.float32
bf16 = jnp.bfloat16
VM = pl.BlockSpec(memory_space=pltpu.VMEM)
SM = pl.BlockSpec(memory_space=pltpu.SMEM)
HB = pl.BlockSpec(memory_space=pl.ANY)


def lane_iota(rows):
    return lax.broadcasted_iota(jnp.int32, (rows, LANES), 1)


def slots(ids):
    expert = lax.broadcasted_iota(jnp.int32, (LANES, ROWS), 0)
    picked = jnp.zeros((LANES, ROWS), f32)
    for k in range(ids.shape[0]):
        picked = picked + jnp.where(ids[k : k + 1, :] == expert, 1.0, 0.0)
    before = lax.broadcasted_iota(jnp.int32, (ROWS, ROWS), 0) < lax.broadcasted_iota(
        jnp.int32, (ROWS, ROWS), 1
    )
    rank = jnp.dot(
        picked.astype(bf16), jnp.where(before, 1.0, 0.0).astype(bf16), preferred_element_type=f32
    )
    first = jnp.where((picked > 0.5) & (rank < 0.5), 1.0, 0.0)
    second = jnp.where((picked > 0.5) & (rank > 0.5) & (rank < 1.5), 1.0, 0.0)
    return first, second


def high_low(values):
    high = values.astype(bf16)
    low = (values - high.astype(f32)).astype(bf16)
    return high, low


def gather_t(onehot, values):
    return lax.dot_general(
        onehot, values, (((0,), (0,)), ((), ())), preferred_element_type=f32
    )


def attend_kernel(
    hidden, queries, cache_key, cache_value, new_key, new_value, lengths, gain, ids,
    source, talk_ids, talk_gates, residual, message, asked, mixed, spread_out, keys, vals, sems,
):
    copies = []
    for i in range(4):
        part = pl.ds(i * 4, 4)
        k_copy = pltpu.make_async_copy(cache_key.at[part], keys.at[part], sems.at[i])
        v_copy = pltpu.make_async_copy(cache_value.at[part], vals.at[part], sems.at[4 + i])
        k_copy.start()
        v_copy.start()
        copies.append((k_copy, v_copy))
    scaling = HEAD_DIM ** (-0.5)
    for h in range(HEADS):
        asked[pl.ds(h, ROWS, stride=HEADS), :] = queries[:, h * 128 : (h + 1) * 128].astype(f32)
    head = lax.broadcasted_iota(jnp.int32, (HEADS, LANES), 0)
    front = head < HEADS // 2
    lane = lane_iota(HEADS)
    fresh_key = new_key[...].astype(f32)
    fresh_value = new_value[...].astype(f32)
    for r in range(ROWS):
        if r % 4 == 0:
            copies[r // 4][0].wait()
            copies[r // 4][1].wait()
        query = asked[r * HEADS : (r + 1) * HEADS, :]
        split = jnp.concatenate(
            [jnp.where(front, query, 0.0), jnp.where(front, 0.0, query)], axis=1
        ).astype(bf16)
        scores = (
            lax.dot_general(
                split, keys[r], (((1,), (1,)), ((), ())), preferred_element_type=f32
            )
            * scaling
        )
        own_key = jnp.where(front, fresh_key[r : r + 1, :128], fresh_key[r : r + 1, 128:])
        own_val = jnp.where(front, fresh_value[r : r + 1, :128], fresh_value[r : r + 1, 128:])
        fresh = jnp.sum(query * own_key, axis=1, keepdims=True) * scaling
        scores = jnp.where(lane < lengths[r], scores, -jnp.inf)
        highest = jnp.maximum(jnp.max(scores, axis=1, keepdims=True), fresh)
        weights = jnp.exp(scores - highest)
        own = jnp.exp(fresh - highest)
        total = jnp.sum(weights, axis=1, keepdims=True) + own
        probs = (weights / total).astype(bf16)
        own_prob = (own / total).astype(bf16).astype(f32)
        both = jnp.dot(probs, vals[r], preferred_element_type=f32)
        mixed[r * HEADS : (r + 1) * HEADS, :] = (
            jnp.where(front, both[:, :128], both[:, 128:]) + own_prob * own_val
        )
    squares = jnp.zeros((ROWS, LANES), f32)
    for h in range(HEADS):
        cols = slice(h * 128, (h + 1) * 128)
        part = hidden[:, cols].astype(f32) + mixed[pl.ds(h, ROWS, stride=HEADS), :]
        residual[:, cols] = part
        squares = squares + part * part
    spread = jnp.sum(squares, axis=1, keepdims=True) * (1.0 / D)
    scale = lax.rsqrt(spread + EPSILON)
    first, second = slots(ids[...])
    both_slots = jnp.concatenate([first, second], axis=0).astype(bf16)
    for h in range(HEADS):
        cols = slice(h * 128, (h + 1) * 128)
        normed = (residual[:, cols] * scale * gain[h : h + 1, :].astype(f32)).astype(bf16)
        sent = jnp.dot(both_slots, normed, preferred_element_type=f32)
        spread_out[pl.ds(h, CHIPS, stride=32), :] = sent[:CHIPS]
        spread_out[pl.ds(HEADS + h, CHIPS, stride=32), :] = sent[CHIPS:]
    message[:, :INFO_ROW, :] = spread_out[...].reshape(CHIPS, 32, LANES).astype(bf16)
    origin = source[...]
    chip = lax.broadcasted_iota(jnp.int32, (CHIPS, ROWS), 0)
    onehot = jnp.where((origin // 32) == chip, 1.0, 0.0).astype(bf16)
    gates = talk_gates[...]
    high = gates.astype(bf16).astype(f32)
    low = gates - high
    fact = lax.broadcasted_iota(jnp.int32, (LANES, ROWS), 0)
    facts = jnp.where(fact == 16 + origin % ROWS, 1.0, 0.0)
    for k in range(2):
        chosen = talk_ids[k : k + 1, :]
        facts = facts + jnp.where(fact == chosen, high[k : k + 1, :], 0.0)
        facts = facts + jnp.where(fact == chosen + 8, low[k : k + 1, :], 0.0)
    told = lax.dot_general(
        onehot, facts.astype(bf16), (((1,), (1,)), ((), ())), preferred_element_type=f32
    )
    message[:, INFO_ROW:, :] = jnp.broadcast_to(
        told.reshape(CHIPS, 1, LANES), (CHIPS, MSG - INFO_ROW, LANES)
    ).astype(bf16)


def silu(x):
    return x * jax.nn.sigmoid(x)


def restore_kernel(gs0, us0, ds0, gs1, us1, ds1, g0, u0, d0, g1, u1, d1, gw, uw, dw):
    i = pl.program_id(0)
    for half, (gs, us, ds, g, u, d) in enumerate(
        [(gs0, us0, ds0, g0, u0, d0), (gs1, us1, ds1, g1, u1, d1)]
    ):
        for j in range(FH // BLK):
            cols = slice(j * BLK, (j + 1) * BLK)
            there = slice(half * FH + j * BLK, half * FH + (j + 1) * BLK)
            gw[:, there] = (g[0, :, cols].astype(f32) * gs[j, 0, i]).astype(bf16)
            uw[:, there] = (u[0, :, cols].astype(f32) * us[j, 0, i]).astype(bf16)
            dw[there, :] = (d[0, cols, :].astype(f32) * ds[j, 0, i]).astype(bf16)


def expert_kernel(
    arrived, g, u, d, produced, info, wide_in, rows_in, gw, uw, dw, out32, sems,
):
    copies = []
    for i, (src, dst) in enumerate([(g, gw), (u, uw), (d, dw)]):
        copy = pltpu.make_async_copy(src, dst, sems.at[i])
        copy.start()
        copies.append(copy)
    wide_in[...] = arrived[...].astype(f32).reshape(CHIPS * MSG, LANES)
    info[...] = wide_in[pl.ds(INFO_ROW, CHIPS, stride=MSG), :].astype(bf16)
    for s in range(2):
        for h in range(HEADS):
            rows_in[s * CHIPS : (s + 1) * CHIPS, h * 128 : (h + 1) * 128] = wide_in[
                pl.ds(s * HEADS + h, CHIPS, stride=MSG), :
            ].astype(bf16)
    copies[0].wait()
    gated = jnp.dot(rows_in[...], gw[...], preferred_element_type=f32)
    copies[1].wait()
    lifted = jnp.dot(rows_in[...], uw[...], preferred_element_type=f32)
    middle = (silu(gated) * lifted).astype(bf16)
    copies[2].wait()
    for h in range(HEADS // 2):
        part = jnp.dot(middle, dw[:, h * 256 : (h + 1) * 256], preferred_element_type=f32)
        for s in range(2):
            for k in range(2):
                spot = pl.ds(s * HEADS + 2 * h + k, CHIPS, stride=32)
                out32[spot, :] = part[s * CHIPS : (s + 1) * CHIPS, k * 128 : (k + 1) * 128]
    produced[...] = out32[...].reshape(CHIPS, 32, LANES).astype(bf16)


def combine_kernel(
    returned, residual, ids, gates, info, gain, thinker_out, onward, wide_in, rows_in,
):
    wide_in[...] = returned[...].astype(f32).reshape(CHIPS * 32, LANES)
    for s in range(2):
        for h in range(HEADS):
            rows_in[s * CHIPS : (s + 1) * CHIPS, h * 128 : (h + 1) * 128] = wide_in[
                pl.ds(s * HEADS + h, CHIPS, stride=32), :
            ].astype(bf16)
    expert = lax.broadcasted_iota(jnp.int32, (LANES, ROWS), 0)
    weight = jnp.zeros((LANES, ROWS), f32)
    for k in range(8):
        weight = weight + jnp.where(ids[k : k + 1, :] == expert, gates[k : k + 1, :], 0.0)
    first, second = slots(ids[...])
    high, low = high_low(jnp.concatenate([first * weight, second * weight], axis=0))
    both = gather_t(jnp.concatenate([high, low], axis=1), rows_in[...])
    routed = both[:ROWS] + both[ROWS:]
    outcome = (residual[...] + routed).astype(bf16)
    thinker_out[...] = outcome
    values = outcome.astype(f32)
    spread = jnp.sum(values * values, axis=1, keepdims=True) * (1.0 / D)
    scale = lax.rsqrt(spread + EPSILON)
    for h in range(HEADS):
        cols = slice(h * 128, (h + 1) * 128)
        onward[:, cols] = (values[:, cols] * scale * gain[h : h + 1, :].astype(f32)).astype(bf16)
    lane = lane_iota(ROWS)
    told = info[...]
    pick = jnp.where(
        lane == 16 + lax.broadcasted_iota(jnp.int32, (ROWS, LANES), 0), 1.0, 0.0
    ).astype(bf16)
    goal = lax.dot_general(
        pick, told, (((1,), (1,)), ((), ())), preferred_element_type=f32
    ).astype(bf16)
    onward[:, D : D + LANES] = goal
    onward[:, D + LANES :] = jnp.dot(goal, told, preferred_element_type=f32).astype(bf16)


def talker_kernel(
    place, m0, m1, m2, m3, g0, u0, d0, g1, u1, d1, relayed, rows_in, gw, uw, dw, out32, sems,
):
    copies = []
    for i, (src, dst) in enumerate(
        [
            (g0, gw.at[0]), (u0, uw.at[0]), (d0, dw.at[0]),
            (g1, gw.at[1]), (u1, uw.at[1]), (d1, dw.at[1]),
        ]
    ):
        copy = pltpu.make_async_copy(src.at[0], dst, sems.at[i])
        copy.start()
        copies.append(copy)
    for i, m in enumerate([m0, m1, m2, m3]):
        rows_in[i * ROWS : (i + 1) * ROWS, :] = m[...]
    inputs = rows_in[:, :D]
    goal = rows_in[:, D : D + LANES]
    shares = rows_in[:, D + LANES :].astype(f32)
    lane = lane_iota(4 * ROWS)
    total = jnp.zeros((4 * ROWS, TD), f32)
    for half in range(2):
        expert = place[0] if half == 0 else place[0] + 1 - 2 * (place[0] % 2)
        share = jnp.sum(
            jnp.where((lane == expert) | (lane == expert + 8), shares, 0.0), axis=1, keepdims=True
        )
        copies[3 * half].wait()
        gated = jnp.dot(inputs, gw[half], preferred_element_type=f32)
        copies[3 * half + 1].wait()
        lifted = jnp.dot(inputs, uw[half], preferred_element_type=f32)
        middle = (silu(gated) * lifted).astype(bf16)
        copies[3 * half + 2].wait()
        part = jnp.dot(middle, dw[half], preferred_element_type=f32)
        total = total + share * part.astype(bf16).astype(f32)
    total = total.astype(bf16)
    for h in range(TD // 128):
        out32[pl.ds(h, CHIPS, stride=8), :] = gather_t(goal, total[:, h * 128 : (h + 1) * 128])
    relayed[...] = out32[...].reshape(CHIPS, 8, LANES).astype(bf16)


def settle_kernel(returned, source, talker_out, wide_in):
    wide_in[...] = returned[...].astype(f32).reshape(CHIPS * 8, LANES)
    chip = lax.broadcasted_iota(jnp.int32, (CHIPS, ROWS), 0)
    onehot = jnp.where((chip // 4) == (source[...] // 128), 1.0, 0.0).astype(bf16)
    for h in range(TD // 128):
        rows = wide_in[pl.ds(h, CHIPS, stride=8), :].astype(bf16)
        talker_out[:, h * 128 : (h + 1) * 128] = gather_t(onehot, rows).astype(bf16)


def sds(shape, dtype):
    return jax.ShapeDtypeStruct(shape, dtype)


def swap(value):
    return lax.ppermute(value, "c", [(0, 1), (1, 0)])


def spread_chips(value):
    return lax.all_to_all(value, ("z", "x", "y"), 0, 0, tiled=True)


def local(
    hidden_in, queries, cache_key, cache_value, new_key, new_value, lengths, norm_gain,
    gate_codes, gate_scale, up_codes, up_scale, down_codes, down_scale, think_ids, think_gates,
    talker_source, talker_gain, talk_gate_w, talk_up_w, talk_down_w, talk_ids, talk_gates,
):
    own = (gate_codes, up_codes, down_codes)
    own_scale = (
        jnp.transpose(gate_scale, (2, 0, 1)),
        jnp.transpose(up_scale, (2, 0, 1)),
        jnp.transpose(down_scale, (1, 0, 2)),
    )
    other = tuple(swap(w) for w in own)
    other_scale = tuple(swap(s) for s in own_scale)
    source = talker_source.reshape(1, ROWS)
    ids = think_ids.T

    residual, message = pl.pallas_call(
        attend_kernel,
        out_shape=(sds((ROWS, D), f32), sds((CHIPS, MSG, LANES), bf16)),
        in_specs=[VM] * 2 + [HB] * 2 + [VM] * 2 + [SM] + [VM] * 5,
        out_specs=(VM, VM),
        scratch_shapes=[
            pltpu.VMEM((ROWS * HEADS, LANES), f32),
            pltpu.VMEM((ROWS * HEADS, LANES), f32),
            pltpu.VMEM((CHIPS * 32, LANES), f32),
            pltpu.VMEM((ROWS, CTX, 256), bf16),
            pltpu.VMEM((ROWS, CTX, 256), bf16),
            pltpu.SemaphoreType.DMA((8,)),
        ],
        name="attend",
    )(
        hidden_in, queries, cache_key, cache_value, new_key, new_value, lengths,
        norm_gain.reshape(HEADS, LANES), ids, source, talk_ids.T, talk_gates.T,
    )
    arrived = spread_chips(message)
    tall = pl.BlockSpec((1, BLK, FH), lambda i: (0, i, 0))
    flat = pl.BlockSpec((1, FH, BLK), lambda i: (0, 0, i))
    tall_out = pl.BlockSpec((BLK, 2 * FH), lambda i: (i, 0))
    flat_out = pl.BlockSpec((2 * FH, BLK), lambda i: (0, i))
    dense = pl.pallas_call(
        restore_kernel,
        grid=(D // BLK,),
        out_shape=(sds((D, 2 * FH), bf16), sds((D, 2 * FH), bf16), sds((2 * FH, D), bf16)),
        in_specs=[SM] * 6 + [tall, tall, flat] * 2,
        out_specs=(tall_out, tall_out, flat_out),
        cost_estimate=pl.CostEstimate(
            flops=6 * D * FH, bytes_accessed=24 * D * FH, transcendentals=0
        ),
        name="restore",
    )(*own_scale, *other_scale, *own, *other)
    produced, info = pl.pallas_call(
        expert_kernel,
        out_shape=(sds((CHIPS, 32, LANES), bf16), sds((CHIPS, LANES), bf16)),
        in_specs=[VM] + [HB] * 3,
        out_specs=(VM, VM),
        scratch_shapes=[
            pltpu.VMEM((CHIPS * MSG, LANES), f32),
            pltpu.VMEM((2 * CHIPS, D), bf16),
            pltpu.VMEM((D, 2 * FH), bf16),
            pltpu.VMEM((D, 2 * FH), bf16),
            pltpu.VMEM((2 * FH, D), bf16),
            pltpu.VMEM((CHIPS * 32, LANES), f32),
            pltpu.SemaphoreType.DMA((3,)),
        ],
        name="experts",
    )(arrived, *dense)
    returned = spread_chips(produced)
    talk_own = (talk_gate_w, talk_up_w, talk_down_w)
    talk_held = lax.optimization_barrier((*talk_own, arrived))[:3]
    talk_other = tuple(swap(w) for w in talk_held)
    thinker_out, onward = pl.pallas_call(
        combine_kernel,
        out_shape=(sds((ROWS, D), bf16), sds((ROWS, TWIDE), bf16)),
        in_specs=[VM] * 6,
        out_specs=(VM, VM),
        scratch_shapes=[
            pltpu.VMEM((CHIPS * 32, LANES), f32),
            pltpu.VMEM((2 * CHIPS, D), bf16),
        ],
        name="combine",
    )(returned, residual, ids, think_gates.T, info, talker_gain.reshape(HEADS, LANES))
    peers = [
        lax.ppermute(onward, "y", [(i, (i + o) % 4) for i in range(4)]) for o in (1, 2, 3)
    ]
    place = (lax.axis_index("y") * 2 + lax.axis_index("c")).astype(jnp.int32).reshape(1)
    relayed = pl.pallas_call(
        talker_kernel,
        out_shape=sds((CHIPS, 8, LANES), bf16),
        in_specs=[SM] + [VM] * 4 + [HB] * 6,
        out_specs=VM,
        scratch_shapes=[
            pltpu.VMEM((4 * ROWS, TWIDE), bf16),
            pltpu.VMEM((2, D, FH), bf16),
            pltpu.VMEM((2, D, FH), bf16),
            pltpu.VMEM((2, FH, TD), bf16),
            pltpu.VMEM((CHIPS * 8, LANES), f32),
            pltpu.SemaphoreType.DMA((6,)),
        ],
        name="talkers",
    )(place, onward, *peers, *talk_own, *talk_other)
    settled = spread_chips(relayed)
    talker_out = pl.pallas_call(
        settle_kernel,
        out_shape=sds((ROWS, TD), bf16),
        in_specs=[VM, VM],
        out_specs=VM,
        scratch_shapes=[pltpu.VMEM((CHIPS * 8, LANES), f32)],
        name="settle",
    )(settled, source)
    return (thinker_out, talker_out)


def solution(mesh):
    fine = Mesh(mesh.devices.reshape(8, 4, 4, 2), ("z", "x", "y", "c"))
    every = ("z", "x", "y", "c")
    two = P(every, None)
    three = P(every, None, None)
    talk = P(("y", "c"), None, None)
    return jax.shard_map(
        local,
        mesh=fine,
        in_specs=(
            two, two, three, three, two, two, P(every), P(),
            three, three, three, three, three, three, two, two,
            P(every), P(), talk, talk, talk, two, two,
        ),
        out_specs=(two, two),
        check_vma=False,
    )
```

```python
import jax
import jax.numpy as jnp
from jax import lax
from jax.experimental import pallas as pl
from jax.experimental.pallas import tpu as pltpu
from jax.sharding import Mesh
from jax.sharding import PartitionSpec as P

HEADS = 16
HEAD_DIM = 128
BLK = 128
CHIPS = 128
LANES = 128
ROWS = 16
CTX = 128
D = 2048
FH = 384
TD = 1024
EPSILON = 1e-06
WIDE = D + LANES
TWIDE = D + 2 * LANES
N_Z = 8
N_XY = 16

f32 = jnp.float32
bf16 = jnp.bfloat16
VM = pl.BlockSpec(memory_space=pltpu.VMEM)
SM = pl.BlockSpec(memory_space=pltpu.SMEM)
HB = pl.BlockSpec(memory_space=pl.ANY)


def lane_iota(rows):
    return lax.broadcasted_iota(jnp.int32, (rows, LANES), 1)


def gather_t(onehot, values):
    return lax.dot_general(
        onehot, values, (((0,), (0,)), ((), ())), preferred_element_type=f32
    )


def attend_kernel(
    hidden, queries, cache_key, cache_value, new_key, new_value, lengths, gain, ids,
    think_gates, source, talk_ids, talk_gates, residual, message, asked, mixed, keys, vals, sems,
):
    copies = []
    for i in range(4):
        part = pl.ds(i * 4, 4)
        k_copy = pltpu.make_async_copy(cache_key.at[part], keys.at[part], sems.at[i])
        v_copy = pltpu.make_async_copy(cache_value.at[part], vals.at[part], sems.at[4 + i])
        k_copy.start()
        v_copy.start()
        copies.append((k_copy, v_copy))
    scaling = HEAD_DIM ** (-0.5)
    for h in range(HEADS):
        asked[pl.ds(h, ROWS, stride=HEADS), :] = queries[:, h * 128 : (h + 1) * 128].astype(f32)
    head = lax.broadcasted_iota(jnp.int32, (HEADS, LANES), 0)
    front = head < HEADS // 2
    lane = lane_iota(HEADS)
    fresh_key = new_key[...].astype(f32)
    fresh_value = new_value[...].astype(f32)
    for r in range(ROWS):
        if r % 4 == 0:
            copies[r // 4][0].wait()
            copies[r // 4][1].wait()
        query = asked[r * HEADS : (r + 1) * HEADS, :]
        split = jnp.concatenate(
            [jnp.where(front, query, 0.0), jnp.where(front, 0.0, query)], axis=1
        ).astype(bf16)
        scores = (
            lax.dot_general(
                split, keys[r], (((1,), (1,)), ((), ())), preferred_element_type=f32
            )
            * scaling
        )
        own_key = jnp.where(front, fresh_key[r : r + 1, :128], fresh_key[r : r + 1, 128:])
        own_val = jnp.where(front, fresh_value[r : r + 1, :128], fresh_value[r : r + 1, 128:])
        fresh = jnp.sum(query * own_key, axis=1, keepdims=True) * scaling
        scores = jnp.where(lane < lengths[r], scores, -jnp.inf)
        highest = jnp.maximum(jnp.max(scores, axis=1, keepdims=True), fresh)
        weights = jnp.exp(scores - highest)
        own = jnp.exp(fresh - highest)
        total = jnp.sum(weights, axis=1, keepdims=True) + own
        probs = (weights / total).astype(bf16)
        own_prob = (own / total).astype(bf16).astype(f32)
        both = jnp.dot(probs, vals[r], preferred_element_type=f32)
        mixed[r * HEADS : (r + 1) * HEADS, :] = (
            jnp.where(front, both[:, :128], both[:, 128:]) + own_prob * own_val
        )
    squares = jnp.zeros((ROWS, LANES), f32)
    for h in range(HEADS):
        cols = slice(h * 128, (h + 1) * 128)
        part = hidden[:, cols].astype(f32) + mixed[pl.ds(h, ROWS, stride=HEADS), :]
        residual[:, cols] = part
        squares = squares + part * part
    spread = jnp.sum(squares, axis=1, keepdims=True) * (1.0 / D)
    scale = lax.rsqrt(spread + EPSILON)
    for h in range(HEADS):
        cols = slice(h * 128, (h + 1) * 128)
        normed = (residual[:, cols] * scale * gain[h : h + 1, :].astype(f32)).astype(bf16)
        for z in range(N_Z):
            message[z, :, cols] = normed
    origin = source[...]
    fact = lax.broadcasted_iota(jnp.int32, (40, ROWS), 0)
    gates = talk_gates[...]
    high = gates.astype(bf16).astype(f32)
    low = gates - high
    facts = jnp.where(fact == 16 + origin % ROWS, 1.0, 0.0)
    facts = facts + jnp.where(fact == 32, (origin // 32).astype(f32), 0.0)
    for k in range(2):
        chosen = talk_ids[k : k + 1, :]
        facts = facts + jnp.where(fact == chosen, high[k : k + 1, :], 0.0)
        facts = facts + jnp.where(fact == chosen + 8, low[k : k + 1, :], 0.0)
    weights = think_gates[...]
    high = weights.astype(bf16).astype(f32)
    low = weights - high
    upright = jnp.concatenate(
        [facts, ids[...].astype(f32), high, low, jnp.zeros((64, ROWS), f32)], axis=0
    ).astype(bf16)
    same = lax.broadcasted_iota(jnp.int32, (ROWS, ROWS), 0) == lax.broadcasted_iota(
        jnp.int32, (ROWS, ROWS), 1
    )
    told = lax.dot_general(
        jnp.where(same, 1.0, 0.0).astype(bf16), upright, (((1,), (1,)), ((), ())),
        preferred_element_type=f32,
    ).astype(bf16)
    for z in range(N_Z):
        message[z, :, D:] = told


def select_kernel(plane, gathered, message, shares):
    rows = N_Z * ROWS
    inputs = gathered[:, :, :D].reshape(rows, D)
    told = gathered[:, :, D:].reshape(rows, LANES)
    facts = told.astype(f32)
    shape = (rows, 2 * LANES)
    col = lax.broadcasted_iota(jnp.int32, shape, 1)
    row = lax.broadcasted_iota(jnp.int32, shape, 0)
    chip = (plane[0] * N_XY + col // 16).astype(f32)
    turn = (col % 16) // 8
    level = (col % 8) == (row // ROWS)
    picked = jnp.zeros(shape, f32)
    high = jnp.zeros(shape, f32)
    low = jnp.zeros(shape, f32)
    for k in range(8):
        match = level & (facts[:, 40 + k : 41 + k] == chip)
        picked = jnp.where(match, 1.0, picked)
        high = jnp.where(match, facts[:, 48 + k : 49 + k], high)
        low = jnp.where(match, facts[:, 56 + k : 57 + k], low)
    below = lax.broadcasted_iota(jnp.int32, (rows, rows), 1) < lax.broadcasted_iota(
        jnp.int32, (rows, rows), 0
    )
    rank = jnp.dot(
        jnp.where(below, 1.0, 0.0).astype(bf16), picked.astype(bf16), preferred_element_type=f32
    )
    chosen = (picked > 0.5) & (jnp.abs(rank - turn.astype(f32)) < 0.5)
    onehot = jnp.where(chosen, 1.0, 0.0).astype(bf16)
    shares[:rows, :] = jnp.where(chosen, high, 0.0).astype(bf16)
    shares[rows:, :] = jnp.where(chosen, low, 0.0).astype(bf16)
    message[:, :, :D] = gather_t(onehot, inputs).astype(bf16).reshape(N_XY, 16, D)
    owned = level & (turn == 0) & (facts[:, 32:33] == chip)
    message[:, :, D:] = (
        gather_t(jnp.where(owned, 1.0, 0.0).astype(bf16), told)
        .astype(bf16)
        .reshape(N_XY, 16, LANES)
    )


def silu(x):
    return x * jax.nn.sigmoid(x)


def restore_kernel(gs0, us0, ds0, gs1, us1, ds1, g0, u0, d0, g1, u1, d1, gw, uw, dw):
    i = pl.program_id(0)
    for half, (gs, us, ds, g, u, d) in enumerate(
        [(gs0, us0, ds0, g0, u0, d0), (gs1, us1, ds1, g1, u1, d1)]
    ):
        for j in range(FH // BLK):
            cols = slice(j * BLK, (j + 1) * BLK)
            there = slice(half * FH + j * BLK, half * FH + (j + 1) * BLK)
            for k in range(2):
                near = slice(k * BLK, (k + 1) * BLK)
                at = 2 * i + k
                gw[near, there] = (g[0, near, cols].astype(f32) * gs[j, 0, at]).astype(bf16)
                uw[near, there] = (u[0, near, cols].astype(f32) * us[j, 0, at]).astype(bf16)
                dw[there, near] = (d[0, cols, near].astype(f32) * ds[j, 0, at]).astype(bf16)


def expert_kernel(arrived, g, u, d, produced, rows_in, gw, uw, dw, sems):
    copies = []
    for i, (src, dst) in enumerate(
        [(arrived.at[:, :, pl.ds(0, D)], rows_in), (g, gw), (u, uw), (d, dw)]
    ):
        copy = pltpu.make_async_copy(src, dst, sems.at[i])
        copy.start()
        copies.append(copy)
    copies[0].wait()
    inputs = rows_in[...].reshape(2 * CHIPS, D)
    copies[1].wait()
    gated = jnp.dot(inputs, gw[...], preferred_element_type=f32)
    copies[2].wait()
    lifted = jnp.dot(inputs, uw[...], preferred_element_type=f32)
    middle = (silu(gated) * lifted).astype(bf16)
    copies[3].wait()
    for h in range(HEADS // 2):
        cols = slice(h * 256, (h + 1) * 256)
        part = jnp.dot(middle, dw[:, cols], preferred_element_type=f32)
        produced[:, :, cols] = part.astype(bf16).reshape(N_XY, 16, 256)


def partial_kernel(returned, shares, partial):
    both = jnp.dot(
        shares[...], returned[...].reshape(2 * CHIPS, D), preferred_element_type=f32
    )
    partial[...] = (both[:CHIPS] + both[CHIPS:]).astype(bf16).reshape(N_Z, ROWS, D)


def combine_kernel(collected, residual, owned, gain, thinker_out, onward):
    routed = residual[...]
    for z in range(N_Z):
        routed = routed + collected[z].astype(f32)
    outcome = routed.astype(bf16)
    thinker_out[...] = outcome
    values = outcome.astype(f32)
    spread = jnp.sum(values * values, axis=1, keepdims=True) * (1.0 / D)
    scale = lax.rsqrt(spread + EPSILON)
    for h in range(HEADS):
        cols = slice(h * 128, (h + 1) * 128)
        onward[:, cols] = (values[:, cols] * scale * gain[h : h + 1, :].astype(f32)).astype(bf16)
    told = owned[...].astype(f32)[:, :8, :].reshape(CHIPS, LANES).astype(bf16)
    pick = jnp.where(
        lane_iota(ROWS) == 16 + lax.broadcasted_iota(jnp.int32, (ROWS, LANES), 0), 1.0, 0.0
    ).astype(bf16)
    goal = lax.dot_general(
        pick, told, (((1,), (1,)), ((), ())), preferred_element_type=f32
    ).astype(bf16)
    onward[:, D : D + LANES] = goal
    onward[:, D + LANES :] = jnp.dot(goal, told, preferred_element_type=f32).astype(bf16)


def talker_kernel(
    place, m0, m1, m2, m3, g0, u0, d0, g1, u1, d1, relayed, rows_in, gw, uw, dw, sems,
):
    copies = []
    for i, (src, dst) in enumerate(
        [
            (g0, gw.at[0]), (u0, uw.at[0]), (d0, dw.at[0]),
            (g1, gw.at[1]), (u1, uw.at[1]), (d1, dw.at[1]),
        ]
    ):
        copy = pltpu.make_async_copy(src.at[0], dst, sems.at[i])
        copy.start()
        copies.append(copy)
    for i, m in enumerate([m0, m1, m2, m3]):
        rows_in[i * ROWS : (i + 1) * ROWS, :] = m[...]
    inputs = rows_in[:, :D]
    goal = rows_in[:, D : D + LANES]
    shares = rows_in[:, D + LANES :].astype(f32)
    lane = lane_iota(4 * ROWS)
    total = jnp.zeros((4 * ROWS, TD), f32)
    for half in range(2):
        expert = place[0] if half == 0 else place[0] + 1 - 2 * (place[0] % 2)
        share = jnp.sum(
            jnp.where((lane == expert) | (lane == expert + 8), shares, 0.0), axis=1, keepdims=True
        )
        copies[3 * half].wait()
        gated = jnp.dot(inputs, gw[half], preferred_element_type=f32)
        copies[3 * half + 1].wait()
        lifted = jnp.dot(inputs, uw[half], preferred_element_type=f32)
        middle = (silu(gated) * lifted).astype(bf16)
        copies[3 * half + 2].wait()
        part = jnp.dot(middle, dw[half], preferred_element_type=f32)
        total = total + share * part.astype(bf16).astype(f32)
    relayed[...] = gather_t(goal, total.astype(bf16)).astype(bf16).reshape(N_XY, 8, TD)


def cross_kernel(returned, relayed):
    line = lax.broadcasted_iota(jnp.int32, (64, CHIPS), 0)
    came = lax.broadcasted_iota(jnp.int32, (64, CHIPS), 1)
    pick = ((line // 8) == (came % 8)) & ((line % 8) == (came // 32))
    out = jnp.dot(
        jnp.where(pick, 1.0, 0.0).astype(bf16), returned[...].reshape(CHIPS, TD),
        preferred_element_type=f32,
    )
    relayed[...] = out.astype(bf16).reshape(N_Z, 8, TD)


def settle_kernel(returned, source, talker_out):
    line = lax.broadcasted_iota(jnp.int32, (64, ROWS), 0)
    wide = source[...] // 128
    pick = ((line // 8) == (wide // 4)) & ((line % 8) == (wide % 4))
    talker_out[...] = gather_t(
        jnp.where(pick, 1.0, 0.0).astype(bf16), returned[...].reshape(64, TD)
    ).astype(bf16)


def sds(shape, dtype):
    return jax.ShapeDtypeStruct(shape, dtype)


def swap(value):
    return lax.ppermute(value, "c", [(0, 1), (1, 0)])


def exchange(value, axes):
    return lax.all_to_all(value, axes, 0, 0, tiled=True)


SMALL = pltpu.CompilerParams(vmem_limit_bytes=24 << 20)


def local(
    hidden_in, queries, cache_key, cache_value, new_key, new_value, lengths, norm_gain,
    gate_codes, gate_scale, up_codes, up_scale, down_codes, down_scale, think_ids, think_gates,
    talker_source, talker_gain, talk_gate_w, talk_up_w, talk_down_w, talk_ids, talk_gates,
):
    own = (gate_codes, up_codes, down_codes)
    own_scale = (
        jnp.transpose(gate_scale, (2, 0, 1)),
        jnp.transpose(up_scale, (2, 0, 1)),
        jnp.transpose(down_scale, (1, 0, 2)),
    )
    other = tuple(swap(w) for w in own)
    other_scale = tuple(swap(s) for s in own_scale)
    source = talker_source.reshape(1, ROWS)

    residual, message = pl.pallas_call(
        attend_kernel,
        out_shape=(sds((ROWS, D), f32), sds((N_Z, ROWS, WIDE), bf16)),
        in_specs=[VM] * 2 + [HB] * 2 + [VM] * 2 + [SM] + [VM] * 6,
        out_specs=(VM, VM),
        scratch_shapes=[
            pltpu.VMEM((ROWS * HEADS, LANES), f32),
            pltpu.VMEM((ROWS * HEADS, LANES), f32),
            pltpu.VMEM((ROWS, CTX, 256), bf16),
            pltpu.VMEM((ROWS, CTX, 256), bf16),
            pltpu.SemaphoreType.DMA((8,)),
        ],
        name="attend",
    )(
        hidden_in, queries, cache_key, cache_value, new_key, new_value, lengths,
        norm_gain.reshape(HEADS, LANES), think_ids.T, think_gates.T, source,
        talk_ids.T, talk_gates.T,
    )
    gathered = exchange(message, "z")
    plane = lax.axis_index("z").astype(jnp.int32).reshape(1)
    chosen, shares = pl.pallas_call(
        select_kernel,
        out_shape=(sds((N_XY, 16, WIDE), bf16), sds((2 * CHIPS, 2 * LANES), bf16)),
        in_specs=[SM, VM],
        out_specs=(VM, VM),
        compiler_params=SMALL,
        name="select",
    )(plane, gathered)
    arrived = exchange(chosen, ("x", "y"))
    tall = pl.BlockSpec((1, 2 * BLK, FH), lambda i: (0, i, 0))
    flat = pl.BlockSpec((1, FH, 2 * BLK), lambda i: (0, 0, i))
    tall_out = pl.BlockSpec((2 * BLK, 2 * FH), lambda i: (i, 0))
    flat_out = pl.BlockSpec((2 * FH, 2 * BLK), lambda i: (0, i))
    dense = pl.pallas_call(
        restore_kernel,
        grid=(D // BLK // 2,),
        out_shape=(sds((D, 2 * FH), bf16), sds((D, 2 * FH), bf16), sds((2 * FH, D), bf16)),
        in_specs=[SM] * 6 + [tall, tall, flat] * 2,
        out_specs=(tall_out, tall_out, flat_out),
        cost_estimate=pl.CostEstimate(
            flops=6 * D * FH, bytes_accessed=24 * D * FH, transcendentals=0
        ),
        name="restore",
    )(*own_scale, *other_scale, *own, *other)
    produced = pl.pallas_call(
        expert_kernel,
        out_shape=sds((N_XY, 16, D), bf16),
        in_specs=[HB] * 4,
        out_specs=VM,
        scratch_shapes=[
            pltpu.VMEM((N_XY, 16, D), bf16),
            pltpu.VMEM((D, 2 * FH), bf16),
            pltpu.VMEM((D, 2 * FH), bf16),
            pltpu.VMEM((2 * FH, D), bf16),
            pltpu.SemaphoreType.DMA((4,)),
        ],
        name="experts",
    )(arrived, *dense)
    returned = exchange(produced, ("x", "y"))
    partial = pl.pallas_call(
        partial_kernel,
        out_shape=sds((N_Z, ROWS, D), bf16),
        in_specs=[VM, VM],
        out_specs=VM,
        compiler_params=SMALL,
        name="partial",
    )(returned, shares)
    collected = exchange(partial, "z")
    talk_own = (talk_gate_w, talk_up_w, talk_down_w)
    talk_held = lax.optimization_barrier((*talk_own, arrived))[:3]
    talk_other = tuple(swap(w) for w in talk_held)
    thinker_out, onward = pl.pallas_call(
        combine_kernel,
        grid=(1,),
        out_shape=(sds((ROWS, D), bf16), sds((ROWS, TWIDE), bf16)),
        in_specs=[
            pl.BlockSpec((N_Z, ROWS, D), lambda i: (0, 0, 0)),
            pl.BlockSpec((ROWS, D), lambda i: (0, 0)),
            pl.BlockSpec((N_XY, 16, LANES), lambda i: (0, 0, D // LANES)),
            pl.BlockSpec((HEADS, LANES), lambda i: (0, 0)),
        ],
        out_specs=(
            pl.BlockSpec((ROWS, D), lambda i: (0, 0)),
            pl.BlockSpec((ROWS, TWIDE), lambda i: (0, 0)),
        ),
        name="combine",
    )(collected, residual, arrived, talker_gain.reshape(HEADS, LANES))
    peers = [
        lax.ppermute(onward, "y", [(i, (i + o) % 4) for i in range(4)]) for o in (1, 2, 3)
    ]
    place = (lax.axis_index("y") * 2 + lax.axis_index("c")).astype(jnp.int32).reshape(1)
    relayed = pl.pallas_call(
        talker_kernel,
        out_shape=sds((N_XY, 8, TD), bf16),
        in_specs=[SM] + [VM] * 4 + [HB] * 6,
        out_specs=VM,
        scratch_shapes=[
            pltpu.VMEM((4 * ROWS, TWIDE), bf16),
            pltpu.VMEM((2, D, FH), bf16),
            pltpu.VMEM((2, D, FH), bf16),
            pltpu.VMEM((2, FH, TD), bf16),
            pltpu.SemaphoreType.DMA((6,)),
        ],
        name="talkers",
    )(place, onward, *peers, *talk_own, *talk_other)
    crossing = exchange(relayed, ("x", "y"))
    crossed = pl.pallas_call(
        cross_kernel,
        out_shape=sds((N_Z, 8, TD), bf16),
        in_specs=[VM],
        out_specs=VM,
        compiler_params=SMALL,
        name="cross",
    )(crossing)
    settled = exchange(crossed, "z")
    talker_out = pl.pallas_call(
        settle_kernel,
        out_shape=sds((ROWS, TD), bf16),
        in_specs=[VM, VM],
        out_specs=VM,
        compiler_params=SMALL,
        name="settle",
    )(settled, source)
    return (thinker_out, talker_out)


def solution(mesh):
    fine = Mesh(mesh.devices.reshape(8, 4, 4, 2), ("z", "x", "y", "c"))
    every = ("z", "x", "y", "c")
    two = P(every, None)
    three = P(every, None, None)
    talk = P(("y", "c"), None, None)
    return jax.shard_map(
        local,
        mesh=fine,
        in_specs=(
            two, two, three, three, two, two, P(every), P(),
            three, three, three, three, three, three, two, two,
            P(every), P(), talk, talk, talk, two, two,
        ),
        out_specs=(two, two),
        check_vma=False,
    )
```

```python
import jax
import jax.numpy as jnp
from jax import lax
from jax.experimental import pallas as pl
from jax.experimental.pallas import tpu as pltpu
from jax.sharding import Mesh
from jax.sharding import PartitionSpec as P

HEADS = 16
HEAD_DIM = 128
BLK = 128
CHIPS = 128
LANES = 128
ROWS = 16
CTX = 128
D = 2048
FH = 384
TD = 1024
EPSILON = 1e-06
WIDE = (D + LANES) // LANES * ROWS
TWIDE = (D + 2 * LANES) // LANES * ROWS
PLAIN = D // LANES * ROWS
N_Z = 8
N_XY = 16

f32 = jnp.float32
bf16 = jnp.bfloat16
VM = pl.BlockSpec(memory_space=pltpu.VMEM)
SM = pl.BlockSpec(memory_space=pltpu.SMEM)
HB = pl.BlockSpec(memory_space=pl.ANY)


def tile(h, rows=ROWS):
    return slice(h * rows, (h + 1) * rows)


def lane_iota(rows):
    return lax.broadcasted_iota(jnp.int32, (rows, LANES), 1)


def gather_t(onehot, values):
    return lax.dot_general(
        onehot, values, (((0,), (0,)), ((), ())), preferred_element_type=f32
    )


def attend_kernel(
    hidden, queries, cache_key, cache_value, new_key, new_value, lengths, gain, ids,
    think_gates, source, talk_ids, talk_gates, residual, message, asked, fresh_key, fresh_value,
    mixed, probs, keys, vals, sems,
):
    k_copy = pltpu.make_async_copy(cache_key, keys, sems.at[0])
    v_copy = pltpu.make_async_copy(cache_value, vals, sems.at[1])
    k_copy.start()
    v_copy.start()
    scaling = HEAD_DIM ** (-0.5)
    for h in range(HEADS):
        spot = pl.ds(h, ROWS, stride=HEADS)
        group = slice(h // 8 * 128, (h // 8 + 1) * 128)
        asked[spot, :] = queries[:, h * 128 : (h + 1) * 128].astype(f32)
        fresh_key[spot, :] = new_key[:, group].astype(f32)
        fresh_value[spot, :] = new_value[:, group].astype(f32)
    front = lax.broadcasted_iota(jnp.int32, (HEADS, LANES), 0) < HEADS // 2
    lane = lane_iota(HEADS)
    fresh = jnp.sum(asked[...] * fresh_key[...], axis=1, keepdims=True) * scaling
    k_copy.wait()
    for r in range(ROWS):
        rows = slice(r * HEADS, (r + 1) * HEADS)
        query = asked[rows, :]
        split = jnp.concatenate(
            [jnp.where(front, query, 0.0), jnp.where(front, 0.0, query)], axis=1
        ).astype(bf16)
        found = lax.dot_general(
            split, keys[r], (((1,), (1,)), ((), ())), preferred_element_type=f32
        )
        mixed[rows, :] = jnp.where(lane < lengths[r], found * scaling, -jnp.inf)
    scores = mixed[...]
    highest = jnp.maximum(jnp.max(scores, axis=1, keepdims=True), fresh)
    weights = jnp.exp(scores - highest)
    own = jnp.exp(fresh - highest)
    total = jnp.sum(weights, axis=1, keepdims=True) + own
    probs[...] = (weights / total).astype(bf16)
    added = (own / total).astype(bf16).astype(f32) * fresh_value[...]
    v_copy.wait()
    for r in range(ROWS):
        rows = slice(r * HEADS, (r + 1) * HEADS)
        both = jnp.dot(probs[rows, :], vals[r], preferred_element_type=f32)
        mixed[rows, :] = jnp.where(front, both[:, :128], both[:, 128:])
    mixed[...] = mixed[...] + added
    squares = jnp.zeros((ROWS, LANES), f32)
    for h in range(HEADS):
        cols = slice(h * 128, (h + 1) * 128)
        part = hidden[:, cols].astype(f32) + mixed[pl.ds(h, ROWS, stride=HEADS), :]
        residual[:, cols] = part
        squares = squares + part * part
    spread = jnp.sum(squares, axis=1, keepdims=True) * (1.0 / D)
    scale = lax.rsqrt(spread + EPSILON)
    for h in range(HEADS):
        cols = slice(h * 128, (h + 1) * 128)
        normed = (residual[:, cols] * scale * gain[h : h + 1, :].astype(f32)).astype(bf16)
        for z in range(N_Z):
            message[z, tile(h), :] = normed
    origin = source[...]
    fact = lax.broadcasted_iota(jnp.int32, (40, ROWS), 0)
    gates = talk_gates[...]
    high = gates.astype(bf16).astype(f32)
    low = gates - high
    facts = jnp.where(fact == 16 + origin % ROWS, 1.0, 0.0)
    facts = facts + jnp.where(fact == 32, (origin // 32).astype(f32), 0.0)
    for k in range(2):
        chosen = talk_ids[k : k + 1, :]
        facts = facts + jnp.where(fact == chosen, high[k : k + 1, :], 0.0)
        facts = facts + jnp.where(fact == chosen + 8, low[k : k + 1, :], 0.0)
    weights = think_gates[...]
    high = weights.astype(bf16).astype(f32)
    low = weights - high
    upright = jnp.concatenate(
        [facts, ids[...].astype(f32), high, low, jnp.zeros((64, ROWS), f32)], axis=0
    ).astype(bf16)
    same = lax.broadcasted_iota(jnp.int32, (ROWS, ROWS), 0) == lax.broadcasted_iota(
        jnp.int32, (ROWS, ROWS), 1
    )
    told = lax.dot_general(
        jnp.where(same, 1.0, 0.0).astype(bf16), upright, (((1,), (1,)), ((), ())),
        preferred_element_type=f32,
    ).astype(bf16)
    for z in range(N_Z):
        message[z, tile(HEADS), :] = told


def select_kernel(plane, ready, gathered, message, shares, inputs):
    rows = N_Z * ROWS
    for h in range(HEADS):
        inputs[:, h * 128 : (h + 1) * 128] = gathered[:, tile(h), :].reshape(rows, LANES)
    told = gathered[:, tile(HEADS), :].reshape(rows, LANES)
    facts = told.astype(f32)
    shape = (rows, 2 * LANES)
    col = lax.broadcasted_iota(jnp.int32, shape, 1)
    row = lax.broadcasted_iota(jnp.int32, shape, 0)
    chip = (plane[0] * N_XY + col // 16).astype(f32)
    turn = (col % 16) // 8
    level = (col % 8) == (row // ROWS)
    picked = jnp.zeros(shape, f32)
    high = jnp.zeros(shape, f32)
    low = jnp.zeros(shape, f32)
    for k in range(8):
        match = level & (facts[:, 40 + k : 41 + k] == chip)
        picked = jnp.where(match, 1.0, picked)
        high = jnp.where(match, facts[:, 48 + k : 49 + k], high)
        low = jnp.where(match, facts[:, 56 + k : 57 + k], low)
    below = lax.broadcasted_iota(jnp.int32, (rows, rows), 1) < lax.broadcasted_iota(
        jnp.int32, (rows, rows), 0
    )
    rank = jnp.dot(
        jnp.where(below, 1.0, 0.0).astype(bf16), picked.astype(bf16), preferred_element_type=f32
    )
    chosen = (picked > 0.5) & (jnp.abs(rank - turn.astype(f32)) < 0.5)
    onehot = jnp.where(chosen, 1.0, 0.0).astype(bf16)
    shares[:rows, :] = jnp.where(chosen, high, 0.0).astype(bf16)
    shares[rows:, :] = jnp.where(chosen, low, 0.0).astype(bf16)
    sent = gather_t(onehot, inputs[...]).astype(bf16)
    for h in range(HEADS):
        message[:, tile(h), :] = sent[:, h * 128 : (h + 1) * 128].reshape(N_XY, 16, LANES)
    owned = level & (turn == 0) & (facts[:, 32:33] == chip)
    message[:, tile(HEADS), :] = (
        gather_t(jnp.where(owned, 1.0, 0.0).astype(bf16), told)
        .astype(bf16)
        .reshape(N_XY, 16, LANES)
    )


def silu(x):
    return x * jax.nn.sigmoid(x)


def scaled(block, scale):
    return (block.astype(f32) * scale).astype(bf16)


def restore_tall_kernel(gs0, us0, gs1, us1, g0, u0, g1, u1, gw, uw, token):
    i = pl.program_id(0)
    token[...] = jnp.zeros_like(token)
    for half, (gs, us, g, u) in enumerate([(gs0, us0, g0, u0), (gs1, us1, g1, u1)]):
        for j in range(FH // BLK):
            cols = slice(j * BLK, (j + 1) * BLK)
            there = slice(half * FH + j * BLK, half * FH + (j + 1) * BLK)
            for k in range(2):
                near = slice(k * BLK, (k + 1) * BLK)
                gw[near, there] = scaled(g[0, near, cols], gs[j, 0, 2 * i + k])
                uw[near, there] = scaled(u[0, near, cols], us[j, 0, 2 * i + k])


def restore_flat_kernel(ds0, ds1, d0, d1, dw):
    i = pl.program_id(0)
    for half, (ds, d) in enumerate([(ds0, d0), (ds1, d1)]):
        for j in range(FH // BLK):
            rows = slice(j * BLK, (j + 1) * BLK)
            there = slice(half * FH + j * BLK, half * FH + (j + 1) * BLK)
            for k in range(4):
                near = slice(k * BLK, (k + 1) * BLK)
                dw[there, near] = scaled(d[0, rows, near], ds[j, 0, 4 * i + k])


def expert_kernel(arrived, g, u, d, produced, wide_in, rows_in, gw, uw, dw, sems):
    copies = []
    for i, (src, dst) in enumerate(
        [(arrived.at[:, pl.ds(0, PLAIN), :], wide_in), (g, gw), (u, uw), (d, dw)]
    ):
        copy = pltpu.make_async_copy(src, dst, sems.at[i])
        copy.start()
        copies.append(copy)
    copies[0].wait()
    for h in range(HEADS):
        rows_in[:, h * 128 : (h + 1) * 128] = wide_in[:, tile(h), :].reshape(2 * CHIPS, LANES)
    inputs = rows_in[...]
    copies[1].wait()
    gated = jnp.dot(inputs, gw[...], preferred_element_type=f32)
    copies[2].wait()
    lifted = jnp.dot(inputs, uw[...], preferred_element_type=f32)
    middle = (silu(gated) * lifted).astype(bf16)
    copies[3].wait()
    for h in range(HEADS // 2):
        cols = slice(h * 256, (h + 1) * 256)
        part = jnp.dot(middle, dw[:, cols], preferred_element_type=f32)
        for k in range(2):
            produced[:, tile(2 * h + k), :] = (
                part[:, k * 128 : (k + 1) * 128].astype(bf16).reshape(N_XY, 16, LANES)
            )


def partial_kernel(returned, shares, partial, rows_in):
    for h in range(HEADS):
        rows_in[:, h * 128 : (h + 1) * 128] = returned[:, tile(h), :].reshape(2 * CHIPS, LANES)
    both = jnp.dot(shares[...], rows_in[...], preferred_element_type=f32)
    total = (both[:CHIPS] + both[CHIPS:]).astype(bf16)
    for h in range(HEADS):
        partial[:, tile(h), :] = total[:, h * 128 : (h + 1) * 128].reshape(N_Z, ROWS, LANES)


def combine_kernel(collected, residual, owned, gain, thinker_out, onward):
    squares = jnp.zeros((ROWS, LANES), f32)
    for h in range(HEADS):
        cols = slice(h * 128, (h + 1) * 128)
        part = residual[:, cols]
        for z in range(N_Z):
            part = part + collected[z, tile(h), :].astype(f32)
        part = part.astype(bf16)
        thinker_out[:, cols] = part
        part = part.astype(f32)
        squares = squares + part * part
    scale = lax.rsqrt(jnp.sum(squares, axis=1, keepdims=True) * (1.0 / D) + EPSILON)
    for h in range(HEADS):
        part = thinker_out[:, h * 128 : (h + 1) * 128].astype(f32)
        onward[tile(h), :] = (part * scale * gain[h : h + 1, :].astype(f32)).astype(bf16)
    told = owned[...].astype(f32)[:, :8, :].reshape(CHIPS, LANES).astype(bf16)
    pick = jnp.where(
        lane_iota(ROWS) == 16 + lax.broadcasted_iota(jnp.int32, (ROWS, LANES), 0), 1.0, 0.0
    ).astype(bf16)
    goal = lax.dot_general(
        pick, told, (((1,), (1,)), ((), ())), preferred_element_type=f32
    ).astype(bf16)
    onward[tile(HEADS), :] = goal
    onward[tile(HEADS + 1), :] = jnp.dot(goal, told, preferred_element_type=f32).astype(bf16)


def talker_kernel(
    place, m0, m1, m2, m3, g0, u0, d0, g1, u1, d1, relayed, rows_in, gw, uw, dw, sems,
):
    copies = []
    for i, (src, dst) in enumerate(
        [
            (g0, gw.at[0]), (u0, uw.at[0]), (d0, dw.at[0]),
            (g1, gw.at[1]), (u1, uw.at[1]), (d1, dw.at[1]),
        ]
    ):
        copy = pltpu.make_async_copy(src.at[0], dst, sems.at[i])
        copy.start()
        copies.append(copy)
    for i, m in enumerate([m0, m1, m2, m3]):
        for h in range(HEADS + 2):
            rows_in[tile(i), h * 128 : (h + 1) * 128] = m[tile(h), :]
    inputs = rows_in[:, :D]
    goal = rows_in[:, D : D + LANES]
    shares = rows_in[:, D + LANES :].astype(f32)
    lane = lane_iota(4 * ROWS)
    total = jnp.zeros((4 * ROWS, TD), f32)
    for half in range(2):
        expert = place[0] if half == 0 else place[0] + 1 - 2 * (place[0] % 2)
        share = jnp.sum(
            jnp.where((lane == expert) | (lane == expert + 8), shares, 0.0), axis=1, keepdims=True
        )
        copies[3 * half].wait()
        gated = jnp.dot(inputs, gw[half], preferred_element_type=f32)
        copies[3 * half + 1].wait()
        lifted = jnp.dot(inputs, uw[half], preferred_element_type=f32)
        middle = (silu(gated) * lifted).astype(bf16)
        copies[3 * half + 2].wait()
        part = jnp.dot(middle, dw[half], preferred_element_type=f32)
        total = total + share * part.astype(bf16).astype(f32)
    sent = gather_t(goal, total.astype(bf16))
    for h in range(TD // 128):
        relayed[:, tile(h, 8), :] = (
            sent[:, h * 128 : (h + 1) * 128].reshape(N_XY, 8, LANES).astype(bf16)
        )


def cross_kernel(returned, relayed):
    line = lax.broadcasted_iota(jnp.int32, (64, CHIPS), 0)
    came = lax.broadcasted_iota(jnp.int32, (64, CHIPS), 1)
    pick = ((line // 8) == (came % 8)) & ((line % 8) == (came // 32))
    pick = jnp.where(pick, 1.0, 0.0).astype(bf16)
    for h in range(TD // 128):
        rows = returned[:, tile(h, 8), :].astype(f32).reshape(CHIPS, LANES).astype(bf16)
        out = jnp.dot(pick, rows, preferred_element_type=f32)
        relayed[:, tile(h, 8), :] = out.reshape(N_Z, 8, LANES).astype(bf16)


def settle_kernel(returned, source, talker_out):
    line = lax.broadcasted_iota(jnp.int32, (64, ROWS), 0)
    wide = source[...] // 128
    pick = ((line // 8) == (wide // 4)) & ((line % 8) == (wide % 4))
    pick = jnp.where(pick, 1.0, 0.0).astype(bf16)
    for h in range(TD // 128):
        rows = returned[:, tile(h, 8), :].astype(f32).reshape(64, LANES).astype(bf16)
        talker_out[:, h * 128 : (h + 1) * 128] = gather_t(pick, rows).astype(bf16)


def sds(shape, dtype):
    return jax.ShapeDtypeStruct(shape, dtype)


def swap(value):
    return lax.ppermute(value, "c", [(0, 1), (1, 0)])


def exchange(value, axes):
    return lax.all_to_all(value, axes, 0, 0, tiled=True)


SMALL = pltpu.CompilerParams(vmem_limit_bytes=24 << 20)


def local(
    hidden_in, queries, cache_key, cache_value, new_key, new_value, lengths, norm_gain,
    gate_codes, gate_scale, up_codes, up_scale, down_codes, down_scale, think_ids, think_gates,
    talker_source, talker_gain, talk_gate_w, talk_up_w, talk_down_w, talk_ids, talk_gates,
):
    own = (gate_codes, up_codes, down_codes)
    own_scale = (
        jnp.transpose(gate_scale, (2, 0, 1)),
        jnp.transpose(up_scale, (2, 0, 1)),
        jnp.transpose(down_scale, (1, 0, 2)),
    )
    other = tuple(swap(w) for w in own)
    other_scale = tuple(swap(s) for s in own_scale)
    source = talker_source.reshape(1, ROWS)

    residual, message = pl.pallas_call(
        attend_kernel,
        out_shape=(sds((ROWS, D), f32), sds((N_Z, WIDE, LANES), bf16)),
        in_specs=[VM] * 2 + [HB] * 2 + [VM] * 2 + [SM] + [VM] * 6,
        out_specs=(VM, VM),
        scratch_shapes=[
            pltpu.VMEM((ROWS * HEADS, LANES), f32),
            pltpu.VMEM((ROWS * HEADS, LANES), f32),
            pltpu.VMEM((ROWS * HEADS, LANES), f32),
            pltpu.VMEM((ROWS * HEADS, LANES), f32),
            pltpu.VMEM((ROWS * HEADS, LANES), bf16),
            pltpu.VMEM((ROWS, CTX, 256), bf16),
            pltpu.VMEM((ROWS, CTX, 256), bf16),
            pltpu.SemaphoreType.DMA((2,)),
        ],
        name="attend",
    )(
        hidden_in, queries, cache_key, cache_value, new_key, new_value, lengths,
        norm_gain.reshape(HEADS, LANES), think_ids.T, think_gates.T, source,
        talk_ids.T, talk_gates.T,
    )
    gathered = exchange(message, "z")
    tall = pl.BlockSpec((1, 2 * BLK, FH), lambda i: (0, i, 0))
    tall_out = pl.BlockSpec((2 * BLK, 2 * FH), lambda i: (i, 0))
    gate_dense, up_dense, token = pl.pallas_call(
        restore_tall_kernel,
        grid=(D // BLK // 2,),
        out_shape=(sds((D, 2 * FH), bf16), sds((D, 2 * FH), bf16), sds((8, LANES), f32)),
        in_specs=[SM] * 4 + [tall] * 4,
        out_specs=(tall_out, tall_out, pl.BlockSpec((8, LANES), lambda i: (0, 0))),
        cost_estimate=pl.CostEstimate(
            flops=4 * D * FH, bytes_accessed=16 * D * FH, transcendentals=0
        ),
        name="restore_tall",
    )(*own_scale[:2], *other_scale[:2], *own[:2], *other[:2])
    flat = pl.BlockSpec((1, FH, 4 * BLK), lambda i: (0, 0, i))
    flat_out = pl.BlockSpec((2 * FH, 4 * BLK), lambda i: (0, i))
    down_dense = pl.pallas_call(
        restore_flat_kernel,
        grid=(D // BLK // 4,),
        out_shape=sds((2 * FH, D), bf16),
        in_specs=[SM] * 2 + [flat] * 2,
        out_specs=flat_out,
        cost_estimate=pl.CostEstimate(
            flops=2 * D * FH, bytes_accessed=8 * D * FH, transcendentals=0
        ),
        name="restore_flat",
    )(own_scale[2], other_scale[2], own[2], other[2])
    plane = lax.axis_index("z").astype(jnp.int32).reshape(1)
    chosen, shares = pl.pallas_call(
        select_kernel,
        out_shape=(sds((N_XY, WIDE, LANES), bf16), sds((2 * CHIPS, 2 * LANES), bf16)),
        in_specs=[SM, HB, VM],
        out_specs=(VM, VM),
        scratch_shapes=[pltpu.VMEM((CHIPS, D), bf16)],
        compiler_params=SMALL,
        name="select",
    )(plane, token, gathered)
    arrived = exchange(chosen, ("x", "y"))
    produced = pl.pallas_call(
        expert_kernel,
        out_shape=sds((N_XY, PLAIN, LANES), bf16),
        in_specs=[HB] * 4,
        out_specs=VM,
        scratch_shapes=[
            pltpu.VMEM((N_XY, PLAIN, LANES), bf16),
            pltpu.VMEM((2 * CHIPS, D), bf16),
            pltpu.VMEM((D, 2 * FH), bf16),
            pltpu.VMEM((D, 2 * FH), bf16),
            pltpu.VMEM((2 * FH, D), bf16),
            pltpu.SemaphoreType.DMA((4,)),
        ],
        name="experts",
    )(arrived, gate_dense, up_dense, down_dense)
    returned = exchange(produced, ("x", "y"))
    partial = pl.pallas_call(
        partial_kernel,
        out_shape=sds((N_Z, PLAIN, LANES), bf16),
        in_specs=[VM, VM],
        out_specs=VM,
        scratch_shapes=[pltpu.VMEM((2 * CHIPS, D), bf16)],
        compiler_params=SMALL,
        name="partial",
    )(returned, shares)
    collected = exchange(partial, "z")
    talk_own = (talk_gate_w, talk_up_w, talk_down_w)
    talk_held = lax.optimization_barrier((*talk_own, arrived))[:3]
    talk_other = tuple(swap(w) for w in talk_held)
    thinker_out, onward = pl.pallas_call(
        combine_kernel,
        grid=(1,),
        out_shape=(sds((ROWS, D), bf16), sds((TWIDE, LANES), bf16)),
        in_specs=[
            pl.BlockSpec((N_Z, PLAIN, LANES), lambda i: (0, 0, 0)),
            pl.BlockSpec((ROWS, D), lambda i: (0, 0)),
            pl.BlockSpec((N_XY, 16, LANES), lambda i: (0, HEADS, 0)),
            pl.BlockSpec((HEADS, LANES), lambda i: (0, 0)),
        ],
        out_specs=(
            pl.BlockSpec((ROWS, D), lambda i: (0, 0)),
            pl.BlockSpec((TWIDE, LANES), lambda i: (0, 0)),
        ),
        name="combine",
    )(collected, residual, arrived, talker_gain.reshape(HEADS, LANES))
    peers = [
        lax.ppermute(onward, "y", [(i, (i + o) % 4) for i in range(4)]) for o in (1, 2, 3)
    ]
    place = (lax.axis_index("y") * 2 + lax.axis_index("c")).astype(jnp.int32).reshape(1)
    relayed = pl.pallas_call(
        talker_kernel,
        out_shape=sds((N_XY, 64, LANES), bf16),
        in_specs=[SM] + [VM] * 4 + [HB] * 6,
        out_specs=VM,
        scratch_shapes=[
            pltpu.VMEM((4 * ROWS, D + 2 * LANES), bf16),
            pltpu.VMEM((2, D, FH), bf16),
            pltpu.VMEM((2, D, FH), bf16),
            pltpu.VMEM((2, FH, TD), bf16),
            pltpu.SemaphoreType.DMA((6,)),
        ],
        name="talkers",
    )(place, onward, *peers, *talk_own, *talk_other)
    crossing = exchange(relayed, ("x", "y"))
    crossed = pl.pallas_call(
        cross_kernel,
        out_shape=sds((N_Z, 64, LANES), bf16),
        in_specs=[VM],
        out_specs=VM,
        compiler_params=SMALL,
        name="cross",
    )(crossing)
    settled = exchange(crossed, "z")
    talker_out = pl.pallas_call(
        settle_kernel,
        out_shape=sds((ROWS, TD), bf16),
        in_specs=[VM, VM],
        out_specs=VM,
        compiler_params=SMALL,
        name="settle",
    )(settled, source)
    return (thinker_out, talker_out)


def solution(mesh):
    fine = Mesh(mesh.devices.reshape(8, 4, 4, 2), ("z", "x", "y", "c"))
    every = ("z", "x", "y", "c")
    two = P(every, None)
    three = P(every, None, None)
    talk = P(("y", "c"), None, None)
    return jax.shard_map(
        local,
        mesh=fine,
        in_specs=(
            two, two, three, three, two, two, P(every), P(),
            three, three, three, three, three, three, two, two,
            P(every), P(), talk, talk, talk, two, two,
        ),
        out_specs=(two, two),
        check_vma=False,
    )
```

```python
import jax
import jax.numpy as jnp
from jax import lax
from jax.experimental import pallas as pl
from jax.experimental.pallas import tpu as pltpu
from jax.sharding import Mesh
from jax.sharding import PartitionSpec as P

HEADS = 16
HEAD_DIM = 128
BLK = 128
CHIPS = 128
LANES = 128
ROWS = 16
CTX = 128
D = 2048
FH = 384
TD = 1024
EPSILON = 1e-06
MSG = 40
INFO_ROW = 32
TWIDE = (D + 2 * LANES) // LANES * ROWS

f32 = jnp.float32
bf16 = jnp.bfloat16
VM = pl.BlockSpec(memory_space=pltpu.VMEM)
SM = pl.BlockSpec(memory_space=pltpu.SMEM)
HB = pl.BlockSpec(memory_space=pl.ANY)


def tile(h, rows=ROWS):
    return slice(h * rows, (h + 1) * rows)


def lane_iota(rows):
    return lax.broadcasted_iota(jnp.int32, (rows, LANES), 1)


def slots(ids):
    expert = lax.broadcasted_iota(jnp.int32, (LANES, ROWS), 0)
    picked = jnp.zeros((LANES, ROWS), f32)
    for k in range(ids.shape[0]):
        picked = picked + jnp.where(ids[k : k + 1, :] == expert, 1.0, 0.0)
    before = lax.broadcasted_iota(jnp.int32, (ROWS, ROWS), 0) < lax.broadcasted_iota(
        jnp.int32, (ROWS, ROWS), 1
    )
    rank = jnp.dot(
        picked.astype(bf16), jnp.where(before, 1.0, 0.0).astype(bf16), preferred_element_type=f32
    )
    first = jnp.where((picked > 0.5) & (rank < 0.5), 1.0, 0.0)
    second = jnp.where((picked > 0.5) & (rank > 0.5) & (rank < 1.5), 1.0, 0.0)
    return first, second


def high_low(values):
    high = values.astype(bf16)
    low = (values - high.astype(f32)).astype(bf16)
    return high, low


def gather_t(onehot, values):
    return lax.dot_general(
        onehot, values, (((0,), (0,)), ((), ())), preferred_element_type=f32
    )


def attend_kernel(
    hidden, queries, cache_key, cache_value, new_key, new_value, lengths, gain, ids, source, talk_ids, talk_gates, residual, message, asked, fresh_key, fresh_value,
    mixed, probs, spread_out, keys, vals, sems,
):
    k_copy = pltpu.make_async_copy(cache_key, keys, sems.at[0])
    v_copy = pltpu.make_async_copy(cache_value, vals, sems.at[1])
    k_copy.start()
    v_copy.start()
    scaling = HEAD_DIM ** (-0.5)
    for h in range(HEADS):
        spot = pl.ds(h, ROWS, stride=HEADS)
        group = slice(h // 8 * 128, (h // 8 + 1) * 128)
        asked[spot, :] = queries[:, h * 128 : (h + 1) * 128].astype(f32)
        fresh_key[spot, :] = new_key[:, group].astype(f32)
        fresh_value[spot, :] = new_value[:, group].astype(f32)
    front = lax.broadcasted_iota(jnp.int32, (HEADS, LANES), 0) < HEADS // 2
    lane = lane_iota(HEADS)
    fresh = jnp.sum(asked[...] * fresh_key[...], axis=1, keepdims=True) * scaling
    k_copy.wait()
    for r in range(ROWS):
        rows = slice(r * HEADS, (r + 1) * HEADS)
        query = asked[rows, :]
        split = jnp.concatenate(
            [jnp.where(front, query, 0.0), jnp.where(front, 0.0, query)], axis=1
        ).astype(bf16)
        found = lax.dot_general(
            split, keys[r], (((1,), (1,)), ((), ())), preferred_element_type=f32
        )
        mixed[rows, :] = jnp.where(lane < lengths[r], found * scaling, -jnp.inf)
    scores = mixed[...]
    highest = jnp.maximum(jnp.max(scores, axis=1, keepdims=True), fresh)
    weights = jnp.exp(scores - highest)
    own = jnp.exp(fresh - highest)
    total = jnp.sum(weights, axis=1, keepdims=True) + own
    probs[...] = (weights / total).astype(bf16)
    added = (own / total).astype(bf16).astype(f32) * fresh_value[...]
    v_copy.wait()
    for r in range(ROWS):
        rows = slice(r * HEADS, (r + 1) * HEADS)
        both = jnp.dot(probs[rows, :], vals[r], preferred_element_type=f32)
        mixed[rows, :] = jnp.where(front, both[:, :128], both[:, 128:])
    mixed[...] = mixed[...] + added
    squares = jnp.zeros((ROWS, LANES), f32)
    for h in range(HEADS):
        cols = slice(h * 128, (h + 1) * 128)
        part = hidden[:, cols].astype(f32) + mixed[pl.ds(h, ROWS, stride=HEADS), :]
        residual[:, cols] = part
        squares = squares + part * part
    spread = jnp.sum(squares, axis=1, keepdims=True) * (1.0 / D)
    scale = lax.rsqrt(spread + EPSILON)
    first, second = slots(ids[...])
    both_slots = jnp.concatenate([first, second], axis=0).astype(bf16)
    for h in range(HEADS // 2):
        pair = []
        for k in range(2):
            cols = slice((2 * h + k) * 128, (2 * h + k + 1) * 128)
            line = gain[2 * h + k : 2 * h + k + 1, :].astype(f32)
            pair.append((residual[:, cols] * scale * line).astype(bf16))
        sent = jnp.dot(both_slots, jnp.concatenate(pair, axis=1), preferred_element_type=f32)
        for k in range(2):
            cols = slice(k * 128, (k + 1) * 128)
            spread_out[pl.ds(2 * h + k, CHIPS, stride=32), :] = sent[:CHIPS, cols]
            spread_out[pl.ds(HEADS + 2 * h + k, CHIPS, stride=32), :] = sent[CHIPS:, cols]
    message[:, :INFO_ROW, :] = spread_out[...].reshape(CHIPS, 32, LANES).astype(bf16)
    origin = source[...]
    chip = lax.broadcasted_iota(jnp.int32, (CHIPS, ROWS), 0)
    onehot = jnp.where((origin // 32) == chip, 1.0, 0.0).astype(bf16)
    gates = talk_gates[...]
    high = gates.astype(bf16).astype(f32)
    low = gates - high
    fact = lax.broadcasted_iota(jnp.int32, (LANES, ROWS), 0)
    facts = jnp.where(fact == 16 + origin % ROWS, 1.0, 0.0)
    for k in range(2):
        chosen = talk_ids[k : k + 1, :]
        facts = facts + jnp.where(fact == chosen, high[k : k + 1, :], 0.0)
        facts = facts + jnp.where(fact == chosen + 8, low[k : k + 1, :], 0.0)
    told = lax.dot_general(
        onehot, facts.astype(bf16), (((1,), (1,)), ((), ())), preferred_element_type=f32
    )
    message[:, INFO_ROW:, :] = jnp.broadcast_to(
        told.reshape(CHIPS, 1, LANES), (CHIPS, MSG - INFO_ROW, LANES)
    ).astype(bf16)


def silu(x):
    return x * jax.nn.sigmoid(x)


def scaled(block, scale):
    return (block.astype(f32) * scale).astype(bf16)


def restore_tall_kernel(gs0, us0, gs1, us1, g0, u0, g1, u1, gw, uw):
    i = pl.program_id(0)
    for half, (gs, us, g, u) in enumerate([(gs0, us0, g0, u0), (gs1, us1, g1, u1)]):
        for j in range(FH // BLK):
            cols = slice(j * BLK, (j + 1) * BLK)
            there = slice(half * FH + j * BLK, half * FH + (j + 1) * BLK)
            for k in range(2):
                near = slice(k * BLK, (k + 1) * BLK)
                gw[near, there] = scaled(g[0, near, cols], gs[j, 0, 2 * i + k])
                uw[near, there] = scaled(u[0, near, cols], us[j, 0, 2 * i + k])


def restore_flat_kernel(ds0, ds1, d0, d1, dw):
    i = pl.program_id(0)
    for half, (ds, d) in enumerate([(ds0, d0), (ds1, d1)]):
        for j in range(FH // BLK):
            rows = slice(j * BLK, (j + 1) * BLK)
            there = slice(half * FH + j * BLK, half * FH + (j + 1) * BLK)
            for k in range(4):
                near = slice(k * BLK, (k + 1) * BLK)
                dw[there, near] = scaled(d[0, rows, near], ds[j, 0, 4 * i + k])


def expert_kernel(arrived, g, u, d, produced, message, wide_in, rows_in, gw, uw, dw, out32, sems):
    copies = []
    for i, (src, dst) in enumerate([(arrived, message), (g, gw), (u, uw), (d, dw)]):
        copy = pltpu.make_async_copy(src, dst, sems.at[i])
        copy.start()
        copies.append(copy)
    copies[0].wait()
    wide_in[...] = message[:, :INFO_ROW, :].astype(f32).reshape(CHIPS * 32, LANES)
    for s in range(2):
        for h in range(HEADS):
            rows_in[s * CHIPS : (s + 1) * CHIPS, h * 128 : (h + 1) * 128] = wide_in[
                pl.ds(s * HEADS + h, CHIPS, stride=32), :
            ].astype(bf16)
    copies[1].wait()
    gated = jnp.dot(rows_in[...], gw[...], preferred_element_type=f32)
    copies[2].wait()
    lifted = jnp.dot(rows_in[...], uw[...], preferred_element_type=f32)
    middle = (silu(gated) * lifted).astype(bf16)
    copies[3].wait()
    for h in range(HEADS // 2):
        part = jnp.dot(middle, dw[:, h * 256 : (h + 1) * 256], preferred_element_type=f32)
        for s in range(2):
            for k in range(2):
                spot = pl.ds(s * HEADS + 2 * h + k, CHIPS, stride=32)
                out32[spot, :] = part[s * CHIPS : (s + 1) * CHIPS, k * 128 : (k + 1) * 128]
    produced[...] = out32[...].reshape(CHIPS, 32, LANES).astype(bf16)


def combine_kernel(
    returned, residual, ids, gates, owned, gain, thinker_out, onward, wide_in, rows_in, facts_in,
):
    wide_in[...] = returned[...].astype(f32).reshape(CHIPS * 32, LANES)
    facts_in[...] = owned[...].astype(f32).reshape(CHIPS * 8, LANES)
    for s in range(2):
        for h in range(HEADS):
            rows_in[s * CHIPS : (s + 1) * CHIPS, h * 128 : (h + 1) * 128] = wide_in[
                pl.ds(s * HEADS + h, CHIPS, stride=32), :
            ].astype(bf16)
    expert = lax.broadcasted_iota(jnp.int32, (LANES, ROWS), 0)
    weight = jnp.zeros((LANES, ROWS), f32)
    for k in range(8):
        weight = weight + jnp.where(ids[k : k + 1, :] == expert, gates[k : k + 1, :], 0.0)
    first, second = slots(ids[...])
    high, low = high_low(jnp.concatenate([first * weight, second * weight], axis=0))
    both = gather_t(jnp.concatenate([high, low], axis=1), rows_in[...])
    outcome = (residual[...] + both[:ROWS] + both[ROWS:]).astype(bf16)
    thinker_out[...] = outcome
    values = outcome.astype(f32)
    scale = lax.rsqrt(
        jnp.sum(values * values, axis=1, keepdims=True) * (1.0 / D) + EPSILON
    )
    for h in range(HEADS):
        part = values[:, h * 128 : (h + 1) * 128]
        onward[tile(h), :] = (part * scale * gain[h : h + 1, :].astype(f32)).astype(bf16)
    told = facts_in[pl.ds(0, CHIPS, stride=8), :].astype(bf16)
    pick = jnp.where(
        lane_iota(ROWS) == 16 + lax.broadcasted_iota(jnp.int32, (ROWS, LANES), 0), 1.0, 0.0
    ).astype(bf16)
    goal = lax.dot_general(
        pick, told, (((1,), (1,)), ((), ())), preferred_element_type=f32
    ).astype(bf16)
    onward[tile(HEADS), :] = goal
    onward[tile(HEADS + 1), :] = jnp.dot(goal, told, preferred_element_type=f32).astype(bf16)


def talker_kernel(
    place, m0, m1, m2, m3, g0, u0, d0, g1, u1, d1, relayed, rows_in, gw, uw, dw, out32, sems,
):
    copies = []
    for i, (src, dst) in enumerate(
        [
            (g0, gw.at[0]), (u0, uw.at[0]), (d0, dw.at[0]),
            (g1, gw.at[1]), (u1, uw.at[1]), (d1, dw.at[1]),
        ]
    ):
        copy = pltpu.make_async_copy(src.at[0], dst, sems.at[i])
        copy.start()
        copies.append(copy)
    for i, m in enumerate([m0, m1, m2, m3]):
        for h in range(HEADS + 2):
            rows_in[tile(i), h * 128 : (h + 1) * 128] = m[tile(h), :]
    inputs = rows_in[:, :D]
    goal = rows_in[:, D : D + LANES]
    shares = rows_in[:, D + LANES :].astype(f32)
    lane = lane_iota(4 * ROWS)
    total = jnp.zeros((4 * ROWS, TD), f32)
    for half in range(2):
        expert = place[0] if half == 0 else place[0] + 1 - 2 * (place[0] % 2)
        share = jnp.sum(
            jnp.where((lane == expert) | (lane == expert + 8), shares, 0.0), axis=1, keepdims=True
        )
        copies[3 * half].wait()
        gated = jnp.dot(inputs, gw[half], preferred_element_type=f32)
        copies[3 * half + 1].wait()
        lifted = jnp.dot(inputs, uw[half], preferred_element_type=f32)
        middle = (silu(gated) * lifted).astype(bf16)
        copies[3 * half + 2].wait()
        part = jnp.dot(middle, dw[half], preferred_element_type=f32)
        total = total + share * part.astype(bf16).astype(f32)
    sent = gather_t(goal, total.astype(bf16))
    for h in range(TD // 128):
        out32[pl.ds(h, CHIPS, stride=8), :] = sent[:, h * 128 : (h + 1) * 128]
    relayed[...] = out32[...].reshape(CHIPS, 8, LANES).astype(bf16)


def settle_kernel(returned, source, talker_out, wide_in):
    wide_in[...] = returned[...].astype(f32).reshape(CHIPS * 8, LANES)
    came = lax.broadcasted_iota(jnp.int32, (CHIPS, ROWS), 0)
    pick = jnp.where((came // 4) == (source[...] // 128), 1.0, 0.0).astype(bf16)
    for h in range(TD // 128):
        rows = wide_in[pl.ds(h, CHIPS, stride=8), :].astype(bf16)
        talker_out[:, h * 128 : (h + 1) * 128] = gather_t(pick, rows).astype(bf16)


def sds(shape, dtype):
    return jax.ShapeDtypeStruct(shape, dtype)


def swap(value):
    return lax.ppermute(value, "c", [(0, 1), (1, 0)])


def exchange(value, axes):
    return lax.all_to_all(value, axes, 0, 0, tiled=True)


CHIP_AXES = ("z", "x", "y")
SMALL = pltpu.CompilerParams(vmem_limit_bytes=24 << 20)


def local(
    hidden_in, queries, cache_key, cache_value, new_key, new_value, lengths, norm_gain,
    gate_codes, gate_scale, up_codes, up_scale, down_codes, down_scale, think_ids, think_gates,
    talker_source, talker_gain, talk_gate_w, talk_up_w, talk_down_w, talk_ids, talk_gates,
):
    own = (gate_codes, up_codes, down_codes)
    own_scale = (
        jnp.transpose(gate_scale, (2, 0, 1)),
        jnp.transpose(up_scale, (2, 0, 1)),
        jnp.transpose(down_scale, (1, 0, 2)),
    )
    other = tuple(swap(w) for w in own)
    other_scale = tuple(swap(s) for s in own_scale)
    source = talker_source.reshape(1, ROWS)

    residual, message = pl.pallas_call(
        attend_kernel,
        out_shape=(sds((ROWS, D), f32), sds((CHIPS, MSG, LANES), bf16)),
        in_specs=[VM] * 2 + [HB] * 2 + [VM] * 2 + [SM] + [VM] * 5,
        out_specs=(VM, VM),
        scratch_shapes=[
            pltpu.VMEM((ROWS * HEADS, LANES), f32),
            pltpu.VMEM((ROWS * HEADS, LANES), f32),
            pltpu.VMEM((ROWS * HEADS, LANES), f32),
            pltpu.VMEM((ROWS * HEADS, LANES), f32),
            pltpu.VMEM((ROWS * HEADS, LANES), bf16),
            pltpu.VMEM((CHIPS * 32, LANES), f32),
            pltpu.VMEM((ROWS, CTX, 256), bf16),
            pltpu.VMEM((ROWS, CTX, 256), bf16),
            pltpu.SemaphoreType.DMA((2,)),
        ],
        name="attend",
    )(
        hidden_in, queries, cache_key, cache_value, new_key, new_value, lengths,
        norm_gain.reshape(HEADS, LANES), think_ids.T, source, talk_ids.T, talk_gates.T,
    )
    arrived = exchange(message, CHIP_AXES)
    tall = pl.BlockSpec((1, 2 * BLK, FH), lambda i: (0, i, 0))
    tall_out = pl.BlockSpec((2 * BLK, 2 * FH), lambda i: (i, 0))
    gate_dense, up_dense = pl.pallas_call(
        restore_tall_kernel,
        grid=(D // BLK // 2,),
        out_shape=(sds((D, 2 * FH), bf16), sds((D, 2 * FH), bf16)),
        in_specs=[SM] * 4 + [tall] * 4,
        out_specs=(tall_out, tall_out),
        cost_estimate=pl.CostEstimate(
            flops=4 * D * FH, bytes_accessed=16 * D * FH, transcendentals=0
        ),
        name="restore_tall",
    )(*own_scale[:2], *other_scale[:2], *own[:2], *other[:2])
    flat = pl.BlockSpec((1, FH, 4 * BLK), lambda i: (0, 0, i))
    flat_out = pl.BlockSpec((2 * FH, 4 * BLK), lambda i: (0, i))
    down_dense = pl.pallas_call(
        restore_flat_kernel,
        grid=(D // BLK // 4,),
        out_shape=sds((2 * FH, D), bf16),
        in_specs=[SM] * 2 + [flat] * 2,
        out_specs=flat_out,
        cost_estimate=pl.CostEstimate(
            flops=2 * D * FH, bytes_accessed=8 * D * FH, transcendentals=0
        ),
        name="restore_flat",
    )(own_scale[2], other_scale[2], own[2], other[2])
    produced = pl.pallas_call(
        expert_kernel,
        out_shape=sds((CHIPS, 32, LANES), bf16),
        in_specs=[HB] * 4,
        out_specs=VM,
        scratch_shapes=[
            pltpu.VMEM((CHIPS, MSG, LANES), bf16),
            pltpu.VMEM((CHIPS * 32, LANES), f32),
            pltpu.VMEM((2 * CHIPS, D), bf16),
            pltpu.VMEM((D, 2 * FH), bf16),
            pltpu.VMEM((D, 2 * FH), bf16),
            pltpu.VMEM((2 * FH, D), bf16),
            pltpu.VMEM((CHIPS * 32, LANES), f32),
            pltpu.SemaphoreType.DMA((4,)),
        ],
        name="experts",
    )(arrived, gate_dense, up_dense, down_dense)
    returned = exchange(produced, CHIP_AXES)
    talk_own = (talk_gate_w, talk_up_w, talk_down_w)
    talk_held = lax.optimization_barrier((*talk_own, arrived))[:3]
    talk_other = tuple(swap(w) for w in talk_held)
    whole = lambda i: (0, 0)
    thinker_out, onward = pl.pallas_call(
        combine_kernel,
        grid=(1,),
        out_shape=(sds((ROWS, D), bf16), sds((TWIDE, LANES), bf16)),
        in_specs=[
            pl.BlockSpec((CHIPS, 32, LANES), lambda i: (0, 0, 0)),
            pl.BlockSpec((ROWS, D), whole),
            pl.BlockSpec((8, ROWS), whole),
            pl.BlockSpec((8, ROWS), whole),
            pl.BlockSpec((CHIPS, 8, LANES), lambda i: (0, INFO_ROW // 8, 0)),
            pl.BlockSpec((HEADS, LANES), whole),
        ],
        out_specs=(pl.BlockSpec((ROWS, D), whole), pl.BlockSpec((TWIDE, LANES), whole)),
        scratch_shapes=[
            pltpu.VMEM((CHIPS * 32, LANES), f32),
            pltpu.VMEM((2 * CHIPS, D), bf16),
            pltpu.VMEM((CHIPS * 8, LANES), f32),
        ],
        name="combine",
    )(
        returned, residual, think_ids.T, think_gates.T, arrived,
        talker_gain.reshape(HEADS, LANES),
    )
    peers = [
        lax.ppermute(onward, "y", [(i, (i + o) % 4) for i in range(4)]) for o in (1, 2, 3)
    ]
    place = (lax.axis_index("y") * 2 + lax.axis_index("c")).astype(jnp.int32).reshape(1)
    relayed = pl.pallas_call(
        talker_kernel,
        out_shape=sds((CHIPS, 8, LANES), bf16),
        in_specs=[SM] + [VM] * 4 + [HB] * 6,
        out_specs=VM,
        scratch_shapes=[
            pltpu.VMEM((4 * ROWS, D + 2 * LANES), bf16),
            pltpu.VMEM((2, D, FH), bf16),
            pltpu.VMEM((2, D, FH), bf16),
            pltpu.VMEM((2, FH, TD), bf16),
            pltpu.VMEM((CHIPS * 8, LANES), f32),
            pltpu.SemaphoreType.DMA((6,)),
        ],
        name="talkers",
    )(place, onward, *peers, *talk_own, *talk_other)
    settled = exchange(relayed, CHIP_AXES)
    talker_out = pl.pallas_call(
        settle_kernel,
        out_shape=sds((ROWS, TD), bf16),
        in_specs=[VM, VM],
        out_specs=VM,
        scratch_shapes=[pltpu.VMEM((CHIPS * 8, LANES), f32)],
        compiler_params=SMALL,
        name="settle",
    )(settled, source)
    return (thinker_out, talker_out)


def solution(mesh):
    fine = Mesh(mesh.devices.reshape(8, 4, 4, 2), ("z", "x", "y", "c"))
    every = ("z", "x", "y", "c")
    two = P(every, None)
    three = P(every, None, None)
    talk = P(("y", "c"), None, None)
    return jax.shard_map(
        local,
        mesh=fine,
        in_specs=(
            two, two, three, three, two, two, P(every), P(),
            three, three, three, three, three, three, two, two,
            P(every), P(), talk, talk, talk, two, two,
        ),
        out_specs=(two, two),
        check_vma=False,
    )
```

```python
import jax
import jax.numpy as jnp
from jax import lax
from jax.experimental import pallas as pl
from jax.experimental.pallas import tpu as pltpu
from jax.sharding import Mesh
from jax.sharding import PartitionSpec as P

HEADS = 16
HEAD_DIM = 128
BLK = 128
CHIPS = 128
LANES = 128
ROWS = 16
CTX = 128
D = 2048
FH = 384
TD = 1024
EPSILON = 1e-06
SLOTS = 2 * CHIPS
TWIDE = (D + 2 * LANES) // LANES * ROWS

f32 = jnp.float32
bf16 = jnp.bfloat16
VM = pl.BlockSpec(memory_space=pltpu.VMEM)
SM = pl.BlockSpec(memory_space=pltpu.SMEM)
HB = pl.BlockSpec(memory_space=pl.ANY)


def tile(h, rows=ROWS):
    return slice(h * rows, (h + 1) * rows)


def lane_iota(rows):
    return lax.broadcasted_iota(jnp.int32, (rows, LANES), 1)


def slots(ids):
    line = lax.broadcasted_iota(jnp.int32, (SLOTS, ROWS), 0)
    picked = jnp.zeros((SLOTS, ROWS), f32)
    for k in range(ids.shape[0]):
        picked = picked + jnp.where(ids[k : k + 1, :] == line // 2, 1.0, 0.0)
    before = lax.broadcasted_iota(jnp.int32, (ROWS, ROWS), 0) < lax.broadcasted_iota(
        jnp.int32, (ROWS, ROWS), 1
    )
    rank = jnp.dot(
        picked.astype(bf16), jnp.where(before, 1.0, 0.0).astype(bf16), preferred_element_type=f32
    )
    turn = (line % 2).astype(f32)
    return jnp.where((picked > 0.5) & (jnp.abs(rank - turn) < 0.5), 1.0, 0.0)


def high_low(values):
    high = values.astype(bf16)
    low = (values - high.astype(f32)).astype(bf16)
    return high, low


def gather_t(onehot, values):
    return lax.dot_general(
        onehot, values, (((0,), (0,)), ((), ())), preferred_element_type=f32
    )


def attend_kernel(
    hidden, queries, cache_key, cache_value, new_key, new_value, lengths, gain, ids, source, talk_ids, talk_gates, residual, message, asked, fresh_key, fresh_value,
    mixed, probs, keys, vals, sems,
):
    k_copy = pltpu.make_async_copy(cache_key, keys, sems.at[0])
    v_copy = pltpu.make_async_copy(cache_value, vals, sems.at[1])
    k_copy.start()
    v_copy.start()
    scaling = HEAD_DIM ** (-0.5)
    for h in range(HEADS):
        spot = pl.ds(h, ROWS, stride=HEADS)
        group = slice(h // 8 * 128, (h // 8 + 1) * 128)
        asked[spot, :] = queries[:, h * 128 : (h + 1) * 128].astype(f32)
        fresh_key[spot, :] = new_key[:, group].astype(f32)
        fresh_value[spot, :] = new_value[:, group].astype(f32)
    front = lax.broadcasted_iota(jnp.int32, (HEADS, LANES), 0) < HEADS // 2
    lane = lane_iota(HEADS)
    fresh = jnp.sum(asked[...] * fresh_key[...], axis=1, keepdims=True) * scaling
    k_copy.wait()
    for r in range(ROWS):
        rows = slice(r * HEADS, (r + 1) * HEADS)
        query = asked[rows, :]
        split = jnp.concatenate(
            [jnp.where(front, query, 0.0), jnp.where(front, 0.0, query)], axis=1
        ).astype(bf16)
        found = lax.dot_general(
            split, keys[r], (((1,), (1,)), ((), ())), preferred_element_type=f32
        )
        mixed[rows, :] = jnp.where(lane < lengths[r], found * scaling, -jnp.inf)
    scores = mixed[...]
    highest = jnp.maximum(jnp.max(scores, axis=1, keepdims=True), fresh)
    weights = jnp.exp(scores - highest)
    own = jnp.exp(fresh - highest)
    total = jnp.sum(weights, axis=1, keepdims=True) + own
    probs[...] = (weights / total).astype(bf16)
    added = (own / total).astype(bf16).astype(f32) * fresh_value[...]
    v_copy.wait()
    for r in range(ROWS):
        rows = slice(r * HEADS, (r + 1) * HEADS)
        both = jnp.dot(probs[rows, :], vals[r], preferred_element_type=f32)
        mixed[rows, :] = jnp.where(front, both[:, :128], both[:, 128:])
    mixed[...] = mixed[...] + added
    squares = jnp.zeros((ROWS, LANES), f32)
    for h in range(HEADS):
        cols = slice(h * 128, (h + 1) * 128)
        part = hidden[:, cols].astype(f32) + mixed[pl.ds(h, ROWS, stride=HEADS), :]
        residual[:, cols] = part
        squares = squares + part * part
    spread = jnp.sum(squares, axis=1, keepdims=True) * (1.0 / D)
    scale = lax.rsqrt(spread + EPSILON)
    both_slots = slots(ids[...]).astype(bf16)
    for h in range(HEADS // 2):
        pair = []
        for k in range(2):
            cols = slice((2 * h + k) * 128, (2 * h + k + 1) * 128)
            line = gain[2 * h + k : 2 * h + k + 1, :].astype(f32)
            pair.append((residual[:, cols] * scale * line).astype(bf16))
        sent = jnp.dot(both_slots, jnp.concatenate(pair, axis=1), preferred_element_type=f32)
        for k in range(2):
            message[:, 2 * h + k, :, :] = (
                sent[:, k * 128 : (k + 1) * 128].astype(bf16).reshape(CHIPS, 2, LANES)
            )
    origin = source[...]
    chip = lax.broadcasted_iota(jnp.int32, (SLOTS, ROWS), 0) // 2
    onehot = jnp.where((origin // 32) == chip, 1.0, 0.0).astype(bf16)
    gates = talk_gates[...]
    high = gates.astype(bf16).astype(f32)
    low = gates - high
    fact = lax.broadcasted_iota(jnp.int32, (LANES, ROWS), 0)
    facts = jnp.where(fact == 16 + origin % ROWS, 1.0, 0.0)
    for k in range(2):
        chosen = talk_ids[k : k + 1, :]
        facts = facts + jnp.where(fact == chosen, high[k : k + 1, :], 0.0)
        facts = facts + jnp.where(fact == chosen + 8, low[k : k + 1, :], 0.0)
    told = lax.dot_general(
        onehot, facts.astype(bf16), (((1,), (1,)), ((), ())), preferred_element_type=f32
    )
    message[:, HEADS, :, :] = told.astype(bf16).reshape(CHIPS, 2, LANES)


def silu(x):
    return x * jax.nn.sigmoid(x)


def scaled(block, scale):
    return (block.astype(f32) * scale).astype(bf16)


def restore_tall_kernel(gs0, us0, gs1, us1, g0, u0, g1, u1, gw, uw):
    i = pl.program_id(0)
    for half, (gs, us, g, u) in enumerate([(gs0, us0, g0, u0), (gs1, us1, g1, u1)]):
        for j in range(FH // BLK):
            cols = slice(j * BLK, (j + 1) * BLK)
            there = slice(half * FH + j * BLK, half * FH + (j + 1) * BLK)
            for k in range(2):
                near = slice(k * BLK, (k + 1) * BLK)
                gw[near, there] = scaled(g[0, near, cols], gs[j, 0, 2 * i + k])
                uw[near, there] = scaled(u[0, near, cols], us[j, 0, 2 * i + k])


def restore_flat_kernel(ds0, ds1, d0, d1, dw):
    i = pl.program_id(0)
    for half, (ds, d) in enumerate([(ds0, d0), (ds1, d1)]):
        for j in range(FH // BLK):
            rows = slice(j * BLK, (j + 1) * BLK)
            there = slice(half * FH + j * BLK, half * FH + (j + 1) * BLK)
            for k in range(4):
                near = slice(k * BLK, (k + 1) * BLK)
                dw[there, near] = scaled(d[0, rows, near], ds[j, 0, 4 * i + k])


def expert_kernel(arrived, g, u, d, produced, message, rows_in, gw, uw, dw, sems):
    copies = []
    for i, (src, dst) in enumerate([(arrived, message), (g, gw), (u, uw), (d, dw)]):
        copy = pltpu.make_async_copy(src, dst, sems.at[i])
        copy.start()
        copies.append(copy)
    copies[0].wait()
    for h in range(HEADS):
        rows_in[:, h * 128 : (h + 1) * 128] = message[:, h, :, :].reshape(SLOTS, LANES)
    copies[1].wait()
    gated = jnp.dot(rows_in[...], gw[...], preferred_element_type=f32)
    copies[2].wait()
    lifted = jnp.dot(rows_in[...], uw[...], preferred_element_type=f32)
    middle = (silu(gated) * lifted).astype(bf16)
    copies[3].wait()
    for h in range(HEADS // 2):
        part = jnp.dot(middle, dw[:, h * 256 : (h + 1) * 256], preferred_element_type=f32)
        for k in range(2):
            produced[:, 2 * h + k, :, :] = (
                part[:, k * 128 : (k + 1) * 128].astype(bf16).reshape(CHIPS, 2, LANES)
            )


def combine_kernel(
    returned, residual, ids, gates, owned, gain, thinker_out, onward, rows_in,
):
    for h in range(HEADS):
        rows_in[:, h * 128 : (h + 1) * 128] = returned[:, h, :, :].reshape(SLOTS, LANES)
    expert = lax.broadcasted_iota(jnp.int32, (SLOTS, ROWS), 0) // 2
    weight = jnp.zeros((SLOTS, ROWS), f32)
    for k in range(8):
        weight = weight + jnp.where(ids[k : k + 1, :] == expert, gates[k : k + 1, :], 0.0)
    high, low = high_low(slots(ids[...]) * weight)
    both = gather_t(jnp.concatenate([high, low], axis=1), rows_in[...])
    outcome = (residual[...] + both[:ROWS] + both[ROWS:]).astype(bf16)
    thinker_out[...] = outcome
    values = outcome.astype(f32)
    scale = lax.rsqrt(
        jnp.sum(values * values, axis=1, keepdims=True) * (1.0 / D) + EPSILON
    )
    for h in range(HEADS):
        part = values[:, h * 128 : (h + 1) * 128]
        onward[tile(h), :] = (part * scale * gain[h : h + 1, :].astype(f32)).astype(bf16)
    line = lax.broadcasted_iota(jnp.int32, (CHIPS, SLOTS), 0)
    even = lax.broadcasted_iota(jnp.int32, (CHIPS, SLOTS), 1) == 2 * line
    told = jnp.dot(
        jnp.where(even, 1.0, 0.0).astype(bf16), owned[:, 0, :, :].reshape(SLOTS, LANES),
        preferred_element_type=f32,
    ).astype(bf16)
    pick = jnp.where(
        lane_iota(ROWS) == 16 + lax.broadcasted_iota(jnp.int32, (ROWS, LANES), 0), 1.0, 0.0
    ).astype(bf16)
    goal = lax.dot_general(
        pick, told, (((1,), (1,)), ((), ())), preferred_element_type=f32
    ).astype(bf16)
    onward[tile(HEADS), :] = goal
    onward[tile(HEADS + 1), :] = jnp.dot(goal, told, preferred_element_type=f32).astype(bf16)


def talker_kernel(
    place, m0, m1, m2, m3, g0, u0, d0, g1, u1, d1, relayed, rows_in, gw, uw, dw, out32, sems,
):
    copies = []
    for i, (src, dst) in enumerate(
        [
            (g0, gw.at[0]), (u0, uw.at[0]), (d0, dw.at[0]),
            (g1, gw.at[1]), (u1, uw.at[1]), (d1, dw.at[1]),
        ]
    ):
        copy = pltpu.make_async_copy(src.at[0], dst, sems.at[i])
        copy.start()
        copies.append(copy)
    for i, m in enumerate([m0, m1, m2, m3]):
        for h in range(HEADS + 2):
            rows_in[tile(i), h * 128 : (h + 1) * 128] = m[tile(h), :]
    inputs = rows_in[:, :D]
    goal = rows_in[:, D : D + LANES]
    shares = rows_in[:, D + LANES :].astype(f32)
    lane = lane_iota(4 * ROWS)
    total = jnp.zeros((4 * ROWS, TD), f32)
    for half in range(2):
        expert = place[0] if half == 0 else place[0] + 1 - 2 * (place[0] % 2)
        share = jnp.sum(
            jnp.where((lane == expert) | (lane == expert + 8), shares, 0.0), axis=1, keepdims=True
        )
        copies[3 * half].wait()
        gated = jnp.dot(inputs, gw[half], preferred_element_type=f32)
        copies[3 * half + 1].wait()
        lifted = jnp.dot(inputs, uw[half], preferred_element_type=f32)
        middle = (silu(gated) * lifted).astype(bf16)
        copies[3 * half + 2].wait()
        part = jnp.dot(middle, dw[half], preferred_element_type=f32)
        total = total + share * part.astype(bf16).astype(f32)
    sent = gather_t(goal, total.astype(bf16))
    for h in range(TD // 128):
        out32[pl.ds(h, CHIPS, stride=8), :] = sent[:, h * 128 : (h + 1) * 128]
    relayed[...] = out32[...].reshape(CHIPS, 8, LANES).astype(bf16)


def settle_kernel(returned, source, talker_out, wide_in):
    wide_in[...] = returned[...].astype(f32).reshape(CHIPS * 8, LANES)
    came = lax.broadcasted_iota(jnp.int32, (CHIPS, ROWS), 0)
    pick = jnp.where((came // 4) == (source[...] // 128), 1.0, 0.0).astype(bf16)
    for h in range(TD // 128):
        rows = wide_in[pl.ds(h, CHIPS, stride=8), :].astype(bf16)
        talker_out[:, h * 128 : (h + 1) * 128] = gather_t(pick, rows).astype(bf16)


def sds(shape, dtype):
    return jax.ShapeDtypeStruct(shape, dtype)


def swap(value):
    return lax.ppermute(value, "c", [(0, 1), (1, 0)])


def exchange(value, axes):
    return lax.all_to_all(value, axes, 0, 0, tiled=True)


CHIP_AXES = ("z", "x", "y")
SMALL = pltpu.CompilerParams(vmem_limit_bytes=24 << 20)


def local(
    hidden_in, queries, cache_key, cache_value, new_key, new_value, lengths, norm_gain,
    gate_codes, gate_scale, up_codes, up_scale, down_codes, down_scale, think_ids, think_gates,
    talker_source, talker_gain, talk_gate_w, talk_up_w, talk_down_w, talk_ids, talk_gates,
):
    own = (gate_codes, up_codes, down_codes)
    own_scale = (
        jnp.transpose(gate_scale, (2, 0, 1)),
        jnp.transpose(up_scale, (2, 0, 1)),
        jnp.transpose(down_scale, (1, 0, 2)),
    )
    other = tuple(swap(w) for w in own)
    other_scale = tuple(swap(s) for s in own_scale)
    source = talker_source.reshape(1, ROWS)

    residual, message = pl.pallas_call(
        attend_kernel,
        out_shape=(sds((ROWS, D), f32), sds((CHIPS, HEADS + 1, 2, LANES), bf16)),
        in_specs=[VM] * 2 + [HB] * 2 + [VM] * 2 + [SM] + [VM] * 5,
        out_specs=(VM, VM),
        scratch_shapes=[
            pltpu.VMEM((ROWS * HEADS, LANES), f32),
            pltpu.VMEM((ROWS * HEADS, LANES), f32),
            pltpu.VMEM((ROWS * HEADS, LANES), f32),
            pltpu.VMEM((ROWS * HEADS, LANES), f32),
            pltpu.VMEM((ROWS * HEADS, LANES), bf16),
            pltpu.VMEM((ROWS, CTX, 256), bf16),
            pltpu.VMEM((ROWS, CTX, 256), bf16),
            pltpu.SemaphoreType.DMA((2,)),
        ],
        name="attend",
    )(
        hidden_in, queries, cache_key, cache_value, new_key, new_value, lengths,
        norm_gain.reshape(HEADS, LANES), think_ids.T, source, talk_ids.T, talk_gates.T,
    )
    arrived = exchange(message, CHIP_AXES)
    tall = pl.BlockSpec((1, 2 * BLK, FH), lambda i: (0, i, 0))
    tall_out = pl.BlockSpec((2 * BLK, 2 * FH), lambda i: (i, 0))
    gate_dense, up_dense = pl.pallas_call(
        restore_tall_kernel,
        grid=(D // BLK // 2,),
        out_shape=(sds((D, 2 * FH), bf16), sds((D, 2 * FH), bf16)),
        in_specs=[SM] * 4 + [tall] * 4,
        out_specs=(tall_out, tall_out),
        cost_estimate=pl.CostEstimate(
            flops=4 * D * FH, bytes_accessed=16 * D * FH, transcendentals=0
        ),
        name="restore_tall",
    )(*own_scale[:2], *other_scale[:2], *own[:2], *other[:2])
    flat = pl.BlockSpec((1, FH, 4 * BLK), lambda i: (0, 0, i))
    flat_out = pl.BlockSpec((2 * FH, 4 * BLK), lambda i: (0, i))
    down_dense = pl.pallas_call(
        restore_flat_kernel,
        grid=(D // BLK // 4,),
        out_shape=sds((2 * FH, D), bf16),
        in_specs=[SM] * 2 + [flat] * 2,
        out_specs=flat_out,
        cost_estimate=pl.CostEstimate(
            flops=2 * D * FH, bytes_accessed=8 * D * FH, transcendentals=0
        ),
        name="restore_flat",
    )(own_scale[2], other_scale[2], own[2], other[2])
    produced = pl.pallas_call(
        expert_kernel,
        out_shape=sds((CHIPS, HEADS, 2, LANES), bf16),
        in_specs=[HB] * 4,
        out_specs=VM,
        scratch_shapes=[
            pltpu.VMEM((CHIPS, HEADS + 1, 2, LANES), bf16),
            pltpu.VMEM((2 * CHIPS, D), bf16),
            pltpu.VMEM((D, 2 * FH), bf16),
            pltpu.VMEM((D, 2 * FH), bf16),
            pltpu.VMEM((2 * FH, D), bf16),
            pltpu.SemaphoreType.DMA((4,)),
        ],
        name="experts",
    )(arrived, gate_dense, up_dense, down_dense)
    returned = exchange(produced, CHIP_AXES)
    talk_own = (talk_gate_w, talk_up_w, talk_down_w)
    talk_held = lax.optimization_barrier((*talk_own, arrived))[:3]
    talk_other = tuple(swap(w) for w in talk_held)
    whole = lambda i: (0, 0)
    thinker_out, onward = pl.pallas_call(
        combine_kernel,
        grid=(1,),
        out_shape=(sds((ROWS, D), bf16), sds((TWIDE, LANES), bf16)),
        in_specs=[
            pl.BlockSpec((CHIPS, HEADS, 2, LANES), lambda i: (0, 0, 0, 0)),
            pl.BlockSpec((ROWS, D), whole),
            pl.BlockSpec((8, ROWS), whole),
            pl.BlockSpec((8, ROWS), whole),
            pl.BlockSpec((CHIPS, 1, 2, LANES), lambda i: (0, HEADS, 0, 0)),
            pl.BlockSpec((HEADS, LANES), whole),
        ],
        out_specs=(pl.BlockSpec((ROWS, D), whole), pl.BlockSpec((TWIDE, LANES), whole)),
        scratch_shapes=[
            pltpu.VMEM((2 * CHIPS, D), bf16),
        ],
        name="combine",
    )(
        returned, residual, think_ids.T, think_gates.T, arrived,
        talker_gain.reshape(HEADS, LANES),
    )
    peers = [
        lax.ppermute(onward, "y", [(i, (i + o) % 4) for i in range(4)]) for o in (1, 2, 3)
    ]
    place = (lax.axis_index("y") * 2 + lax.axis_index("c")).astype(jnp.int32).reshape(1)
    relayed = pl.pallas_call(
        talker_kernel,
        out_shape=sds((CHIPS, 8, LANES), bf16),
        in_specs=[SM] + [VM] * 4 + [HB] * 6,
        out_specs=VM,
        scratch_shapes=[
            pltpu.VMEM((4 * ROWS, D + 2 * LANES), bf16),
            pltpu.VMEM((2, D, FH), bf16),
            pltpu.VMEM((2, D, FH), bf16),
            pltpu.VMEM((2, FH, TD), bf16),
            pltpu.VMEM((CHIPS * 8, LANES), f32),
            pltpu.SemaphoreType.DMA((6,)),
        ],
        name="talkers",
    )(place, onward, *peers, *talk_own, *talk_other)
    settled = exchange(relayed, CHIP_AXES)
    talker_out = pl.pallas_call(
        settle_kernel,
        out_shape=sds((ROWS, TD), bf16),
        in_specs=[VM, VM],
        out_specs=VM,
        scratch_shapes=[pltpu.VMEM((CHIPS * 8, LANES), f32)],
        compiler_params=SMALL,
        name="settle",
    )(settled, source)
    return (thinker_out, talker_out)


def solution(mesh):
    fine = Mesh(mesh.devices.reshape(8, 4, 4, 2), ("z", "x", "y", "c"))
    every = ("z", "x", "y", "c")
    two = P(every, None)
    three = P(every, None, None)
    talk = P(("y", "c"), None, None)
    return jax.shard_map(
        local,
        mesh=fine,
        in_specs=(
            two, two, three, three, two, two, P(every), P(),
            three, three, three, three, three, three, two, two,
            P(every), P(), talk, talk, talk, two, two,
        ),
        out_specs=(two, two),
        check_vma=False,
    )
```
